256 devices in a mesh: batch: 4 (over x_lo, core), ctx: 16 (over x_hi, z), head: 4 (over y).
Axes of the slice: x: 4 (x_hi: 2, x_lo: 2; x = x_hi * 2 + x_lo), y: 4, z: 8, core: 2. Of those that a mesh axis runs over, the one named last changes fastest.
Arguments:
- query_raw: bfloat16 [32768, 2560], P(('batch', 'ctx'), 'head'), parts along dimension 0, may hold values from -400 to 400
- key_raw: bfloat16 [32768, 2560], P(('batch', 'ctx'), 'head'), parts along dimension 0, may hold values from -400 to 400
- value_rows: bfloat16 [32768, 2560], P(('batch', 'ctx'), 'head'), parts along dimension 0, may hold values from -6 to 6
- query_gain: float32 [2560], P('head'), may hold values from 1.2 to 2
- key_gain: float32 [2560], P('head'), may hold values from 1.2 to 2
- segment: int32 [32768], P(('batch', 'ctx')), parts along dimension 0, may hold values from 0 to 5, never falling along the last dimension, each value on 1 to 2048 neighbouring positions
- destination: int32 [32768], P(('batch', 'ctx')), parts along dimension 0, may hold values from 0 to 8191, as said below
- timestep: int32 [24], P('batch'), parts along dimension 0, may hold values from 0 to 49
- out_weight: bfloat16 [2560, 5120], P('head'), may hold values from -0.3125 to 0.3125
- gate_table: float32 [50, 5120], P(None, 'head'), may hold values from 0.5 to 1.5
Outputs:
- gated: bfloat16 [32768, 5120], P(('batch', 'ctx'), 'head'), parts along dimension 0
The draws below stay inside these ranges and needn't reach their ends.
There are 4 independent parts, one for each index of `batch`. The reference program is written for one: setup_inputs(seed, part) draws one part's arguments, and reference() takes and returns one part's arrays. A program takes and returns all parts, laid end to end along the dimension named above; an argument that names none is the same for every part. Nothing has to cross between parts.
Inputs may be any that keep to these rules, and one draw needn't show every extreme that they name: `segment`: the positions of one video are contiguous and the numbers never fall; each of the 6 videos has 1 to 2048 positions, some video exactly 2048. `destination`: A permutation of the 8192 rows. The 512 positions of each block b of 512 go 32 to every block c, and fill rows c*512 + b*32 to c*512 + (b+1)*32 - 1.
All inputs are finite; a program needn't handle non-finite values.
Results may differ from the reference program's by a relative error of at most 0.01555.
Values may be sent and summed in bfloat16 or wider, within the bound.
A program may use at most 192 MiB of HBM per device.

```python
import math
import jax
import jax.numpy as jnp
import numpy as np
from jax import lax

D = 5120
HEADS = 20
HD = 128
STEPS = 50
VIDEOS = 6
TOK_DEV = 512
WIDTH = 2560
TOKENS = 8192
MAXLEN = 2048
N_HEAD = 4


def column_scales(key):
    spread = jax.random.uniform(jax.random.fold_in(key, 11), (WIDTH,), jnp.float32, 0.0, math.log(10.0))
    placing = jnp.arange(WIDTH).astype(jnp.float32) / (WIDTH - 1)
    return jnp.exp(spread + placing * math.log(3.0)) / 3.0


def raw_field(key, which):
    inner_key = jax.random.fold_in(key, which)
    entries = jnp.clip(jax.random.normal(jax.random.fold_in(inner_key, 2), (TOKENS, WIDTH), jnp.float32), -4.0, 4.0)
    row_scale = jnp.exp(jax.random.uniform(jax.random.fold_in(inner_key, 1), (TOKENS, 1), jnp.float32, 0.0, math.log(10.0)))
    return entries * row_scale * column_scales(key)[None, :]


def draw_query_raw(key, part):
    result = raw_field(key, 1)
    return result.astype(jnp.bfloat16)


def draw_key_raw(key, part):
    result = raw_field(key, 2)
    return result.astype(jnp.bfloat16)


def draw_destination(key, part):
    blocks = TOKENS // TOK_DEV
    block_keys = jax.random.split(jax.random.fold_in(key, 5), blocks)
    orders = jax.vmap(lambda one_key: jax.random.permutation(one_key, TOK_DEV))(block_keys)
    slot_count = TOK_DEV // blocks
    sources = jnp.arange(blocks)[:, None]
    targets = orders % blocks
    within = orders // blocks
    result = targets * TOK_DEV + sources * slot_count + within
    return result.reshape(TOKENS).astype(jnp.int32)


def set_ends(values, rng, least, high):
    longest = values.shape.index(max(values.shape))
    spots = []
    for shift in (0, 1):
        where = [jax.random.randint(jax.random.fold_in(rng, axis), (), 0, length) for axis, length in enumerate(values.shape)]
        where[longest] = (where[longest] + shift) % values.shape[longest]
        spots.append(tuple(where))
    return values.at[spots[0]].set(least).at[spots[1]].set(high)


def with_spikes(values, own_key, source, target, parts, factor):
    def block_of(position):
        return (jnp.arange(values.shape[position]) // (values.shape[position] // parts)).reshape((-1,) + (1,) * (values.ndim - 1 - position))

    first = jax.random.permutation(own_key, parts)[block_of(target)]
    far = (block_of(target) + parts // 2) % parts
    return jnp.where((block_of(source) == first) | (block_of(source) == far), factor * values, values)


def steps_of(key, extent, pieces, low, top_value):
    gain = 1.0
    for position, parts in pieces:
        draws = jax.random.uniform(jax.random.fold_in(jax.random.fold_in(key, 6), position), (parts,), jnp.float32, low / len(pieces), top_value / len(pieces))
        gain = gain * jnp.repeat(jnp.exp(draws), extent[position] // parts).reshape((-1,) + (1,) * (len(extent) - 1 - position))
    return gain


def profile(amount, total, most, skew):
    weights = [(1 << 20) // math.isqrt(grade ** skew) + 1 for grade in range(2, amount + 1)]
    rest, given = total - most - (amount - 1), [1] * (amount - 1)
    while rest > 0:
        free = [i for i in range(amount - 1) if given[i] < most]
        pool, left = sum([weights[i] for i in free]), rest
        for i in free:
            more = min(most - given[i], max(1, left * weights[i] // pool), rest)
            given[i] = given[i] + more
            rest = rest - more
    return np.array([most] + given)


def uneven(stream_key, count, total, most, lean):
    if count == 2:
        one = jax.random.randint(stream_key, (), max(1, total - most), min(most, total - 1) + 1)
        return jnp.stack([one, total - one])
    sizes = jnp.asarray(profile(count, total, most, lean), jnp.int32)
    pairs = (count - 1) // 2
    donor, sink = sizes[1:1 + 2 * pairs:2], sizes[2:2 + 2 * pairs:2]
    slack = jnp.minimum(donor - 1, most - sink)
    moved = jax.random.randint(jax.random.fold_in(stream_key, 1), (pairs,), 0, 1 << 20) % (slack + 1)
    sizes = sizes.at[1:1 + 2 * pairs:2].set(donor - moved).at[2:2 + 2 * pairs:2].set(sink + moved)
    return sizes[jax.random.permutation(jax.random.fold_in(stream_key, 2), count)]


def bell_draw(rng, extent, scale, limit, shards=(), kind=jnp.bfloat16):
    values = jax.random.normal(rng, extent, jnp.float32) * scale
    if len(shards) > 0:
        values = steps_of(rng, extent, shards, -0.22, 0.18) * values
    return jnp.clip(values, min=-limit, max=limit).astype(kind)


def heavy_noise(key, shape, width, bound, cuts, heavy, kind=jnp.bfloat16):
    values = width * jax.random.normal(key, shape, jnp.float32)
    if cuts:
        values = values * steps_of(key, shape, cuts, -0.22, 0.18)
    return jnp.clip(with_spikes(values, jax.random.fold_in(key, 3), *heavy), -bound, bound).astype(kind)


def setup_inputs(seed: int = 0, part: int = 0) -> dict:
    key_of = jax.random.split(jax.random.key(seed), 11)
    own_keys = jax.random.split(jax.random.fold_in(key_of[10], part), 11)
    query_raw = draw_query_raw(jax.random.fold_in(jax.random.fold_in(key_of[10], part), 71), part)
    key_raw = draw_key_raw(jax.random.fold_in(jax.random.fold_in(key_of[10], part), 71), part)
    value_rows = bell_draw(own_keys[2], (TOKENS, WIDTH), 1.0, 6.0, ((0, 16), (1, 4)))
    query_gain = jnp.clip(1.2 + 0.79999995 * jax.random.uniform(key_of[3], (WIDTH,), jnp.float32) ** steps_of(key_of[3], (WIDTH,), ((0, 4),), -0.2, 0.2), 1.2, 2.0)
    key_gain = jnp.clip(1.2 + 0.79999995 * jax.random.uniform(key_of[4], (WIDTH,), jnp.float32) ** steps_of(key_of[4], (WIDTH,), ((0, 4),), -0.2, 0.2), 1.2, 2.0)
    segment = jnp.searchsorted(jnp.cumsum(uneven(own_keys[5], VIDEOS, TOKENS, MAXLEN, 2)), jnp.arange(TOKENS), side="right").astype(jnp.int32)
    destination = draw_destination(jax.random.fold_in(jax.random.fold_in(key_of[10], part), 71), part)
    timestep = set_ends(jax.random.randint(own_keys[7], (VIDEOS,), 0, STEPS), jax.random.fold_in(own_keys[7], 1), 0, STEPS - 1).astype(jnp.int32)
    out_weight = heavy_noise(key_of[8], (WIDTH, D), (WIDTH // 4) ** -0.5, 0.3125, ((0, 4),), (0, 1, 4, 2.0))
    gate_table = jnp.clip(0.5 + 1.0 * jax.random.uniform(key_of[9], (STEPS, D), jnp.float32) ** steps_of(key_of[9], (STEPS, D), ((1, 4),), -0.2, 0.2), 0.5, 1.5)
    return {"query_raw": query_raw, "key_raw": key_raw, "value_rows": value_rows, "query_gain": query_gain, "key_gain": key_gain, "segment": segment, "destination": destination, "timestep": timestep, "out_weight": out_weight, "gate_table": gate_table}


def normalize(raw_rows, gain_row):
    floats = raw_rows.astype(jnp.float32)
    mean_square = lax.optimization_barrier(jnp.mean(floats * floats, axis=1, keepdims=True))
    return (floats * lax.rsqrt(mean_square + 1e-06) * gain_row).astype(jnp.bfloat16)

def reference(query_raw, key_raw, value_rows, query_gain, key_gain, segment, destination, timestep, out_weight, gate_table):
    queries = normalize(query_raw, query_gain)
    normed_keys = normalize(key_raw, key_gain)
    score_scale = 1.0 / math.sqrt(HD)
    query_heads = queries.astype(jnp.float32).reshape(TOKENS, HEADS, HD)
    key_heads = normed_keys.astype(jnp.float32).reshape(TOKENS, HEADS, HD)
    value_heads = value_rows.astype(jnp.float32).reshape(TOKENS, HEADS, HD)
    block_rows = min(TOK_DEV, 256)

    def attend_block(first_row):
        block_queries = lax.dynamic_slice_in_dim(query_heads, first_row, block_rows, 0)
        block_marks = lax.dynamic_slice_in_dim(segment, first_row, block_rows, 0)
        scores = jnp.einsum('qhd,khd->hqk', block_queries, key_heads) * score_scale
        allowed = (block_marks[:, None] == segment[None, :])[None]
        scores = jnp.where(allowed, scores, -jnp.inf)
        largest = lax.optimization_barrier(jnp.max(scores, axis=2, keepdims=True))
        exponent = jnp.exp(scores - largest)
        totals = lax.optimization_barrier(jnp.sum(exponent, axis=2))
        weights = lax.optimization_barrier(exponent.astype(jnp.bfloat16)).astype(jnp.float32)
        output = jnp.einsum('hqk,khd->qhd', weights, value_heads) / jnp.transpose(totals)[:, :, None]
        return output.reshape(block_rows, HEADS * HD).astype(jnp.bfloat16)
    starts = (jnp.arange(TOKENS // block_rows) * block_rows).astype(jnp.int32)
    attended = lax.map(attend_block, starts).reshape(TOKENS, HEADS * HD)
    group_width = HEADS * HD // N_HEAD
    mixed_rows = jnp.zeros((TOKENS, D), jnp.float32)
    for member in range(N_HEAD):
        partial_value = jnp.dot(attended[:, member * group_width:(member + 1) * group_width], out_weight[member * group_width:(member + 1) * group_width], preferred_element_type=jnp.float32)
        mixed_rows = mixed_rows + lax.optimization_barrier(partial_value.astype(jnp.bfloat16)).astype(jnp.float32)
    owned = jnp.zeros_like(mixed_rows).at[destination].set(mixed_rows)
    owned_video = jnp.zeros_like(segment).at[destination].set(segment)
    video_gates = jnp.dot(jax.nn.one_hot(timestep, STEPS, dtype=jnp.float32), gate_table, precision=lax.Precision.HIGHEST)
    token_gates = jnp.dot(jax.nn.one_hot(owned_video, VIDEOS, dtype=jnp.float32), video_gates, precision=lax.Precision.HIGHEST)
    return (owned * token_gates).astype(jnp.bfloat16)
```

```python
import functools
import math

import jax
import jax.numpy as jnp
from jax import lax
from jax.experimental import pallas as pl
from jax.experimental.pallas import tpu as pltpu
from jax.sharding import PartitionSpec as P

HD = 128
REACH = 4


def flash_kernel(
    need_ref, qp_ref, kt_ref, kp_ref,
    q_ref, k_ref, v_ref, qs_ref, ks_ref,
    o_ref, m_scr, l_scr, acc_scr, *, offsets, score_scale
):
    j = pl.program_id(0)
    o = pl.program_id(1)

    @pl.when(o == 0)
    def _():
        m_scr[...] = jnp.full_like(m_scr, -1e30)
        l_scr[...] = jnp.zeros_like(l_scr)
        acc_scr[...] = jnp.zeros_like(acc_scr)

    @pl.when(need_ref[j * offsets + o] != 0)
    def _():
        q = q_ref[0]
        k = k_ref[0]
        s = lax.dot_general(
            q, k, (((1,), (1,)), ((), ())), preferred_element_type=jnp.float32
        ) * score_scale
        mask = qs_ref[0] == ks_ref[0]
        s = jnp.where(mask, s, -1e30)
        m_prev = m_scr[...]
        m_new = jnp.maximum(m_prev, jnp.max(s, axis=1, keepdims=True))
        alpha = jnp.exp(m_prev - m_new)
        p = jnp.where(mask, jnp.exp(s - m_new), 0.0)
        l_scr[...] = alpha * l_scr[...] + jnp.sum(p, axis=1, keepdims=True)
        acc_scr[...] = alpha * acc_scr[...] + jnp.dot(
            p.astype(jnp.bfloat16), v_ref[0], preferred_element_type=jnp.float32
        )
        m_scr[...] = m_new

    @pl.when(o == offsets - 1)
    def _():
        o_ref[0] = (acc_scr[...] / l_scr[...]).astype(o_ref.dtype)


def flash(need, qp, kt, kp, q_tiles, k_tiles, v_tiles, seg_rows, seg_cols, score_scale):
    slots, rows, width = q_tiles.shape
    offsets = 2 * REACH + 1
    kern = functools.partial(flash_kernel, offsets=offsets, score_scale=score_scale)
    grid_spec = pltpu.PrefetchScalarGridSpec(
        num_scalar_prefetch=4,
        grid=(slots, offsets),
        in_specs=[
            pl.BlockSpec((1, rows, width), lambda j, o, nd, qp, kt, kp: (j, 0, 0)),
            pl.BlockSpec((1, rows, width), lambda j, o, nd, qp, kt, kp: (kt[j * offsets + o], 0, 0)),
            pl.BlockSpec((1, rows, width), lambda j, o, nd, qp, kt, kp: (kt[j * offsets + o], 0, 0)),
            pl.BlockSpec((1, rows, 1), lambda j, o, nd, qp, kt, kp: (qp[j], 0, 0)),
            pl.BlockSpec((1, 1, rows), lambda j, o, nd, qp, kt, kp: (kp[j * offsets + o], 0, 0)),
        ],
        out_specs=pl.BlockSpec((1, rows, width), lambda j, o, nd, qp, kt, kp: (j, 0, 0)),
        scratch_shapes=[
            pltpu.VMEM((rows, 1), jnp.float32),
            pltpu.VMEM((rows, 1), jnp.float32),
            pltpu.VMEM((rows, width), jnp.float32),
        ],
    )
    return pl.pallas_call(
        kern,
        grid_spec=grid_spec,
        out_shape=jax.ShapeDtypeStruct((slots, rows, width), jnp.bfloat16),
        compiler_params=pltpu.CompilerParams(
            dimension_semantics=("arbitrary", "arbitrary")
        ),
    )(need, qp, kt, kp, q_tiles, k_tiles, v_tiles, seg_rows, seg_cols)


def local(
    query_raw,
    key_raw,
    value_rows,
    query_gain,
    key_gain,
    segment,
    destination,
    timestep,
    out_weight,
    gate_table,
):
    row_count = query_raw.shape[0]
    row_width = query_raw.shape[1]
    head_count = row_width // HD
    ctx_size = lax.axis_size("ctx")
    total_width = row_width * lax.axis_size("head")
    score_scale = 1.0 / math.sqrt(HD)
    me = lax.axis_index("ctx")
    tiles = head_count * ctx_size
    slots = tiles // ctx_size

    query_float = query_raw.astype(jnp.float32)
    key_float = key_raw.astype(jnp.float32)
    query_sum, key_sum = lax.psum(
        (jnp.sum(query_float * query_float, axis=1), jnp.sum(key_float * key_float, axis=1)), "head"
    )
    queries = (
        query_float * lax.rsqrt(query_sum / total_width + 1e-06)[:, None] * query_gain
    ).astype(jnp.bfloat16)
    normed_keys = (key_float * lax.rsqrt(key_sum / total_width + 1e-06)[:, None] * key_gain).astype(
        jnp.bfloat16
    )

    qkv = jnp.stack([queries, normed_keys, value_rows]).reshape(3, row_count, head_count, HD)
    qkv = jnp.transpose(qkv, (0, 2, 1, 3))

    inverse = pow(slots, -1, ctx_size)
    own = []
    for j in range(slots):
        target = lax.rem(inverse * (me - j + ctx_size), ctx_size)
        head = (slots * target + j) // ctx_size
        piece = lax.dynamic_index_in_dim(qkv, head, axis=1, keepdims=False)
        perm = [((slots * e + j) % ctx_size, e) for e in range(ctx_size)]
        own.append(lax.ppermute(piece, "ctx", perm))
    own = jnp.stack(own, axis=1)

    kv_own = own[1:]
    left = lax.ppermute(
        kv_own[:, slots - REACH:], "ctx", [(e, e + 1) for e in range(ctx_size - 1)]
    )
    right = lax.ppermute(
        kv_own[:, :REACH], "ctx", [(e, e - 1) for e in range(1, ctx_size)]
    )
    kv_all = jnp.concatenate([left, kv_own, right], axis=1)

    seg_all = lax.all_gather(segment, "ctx", axis=0, tiled=True)
    dest_all = lax.all_gather(destination, "ctx", axis=0, tiled=True)
    seg_blocks = seg_all.reshape(ctx_size, row_count)
    seg_lo = seg_blocks[:, 0]
    seg_hi = seg_blocks[:, -1]

    offsets = 2 * REACH + 1
    jj = jnp.arange(slots, dtype=jnp.int32)[:, None]
    oo = jnp.arange(offsets, dtype=jnp.int32)[None, :] - REACH
    t_q = slots * me + jj
    t_k = t_q + oo
    p_q = t_q % ctx_size
    valid = (t_k >= 0) & (t_k < tiles)
    t_kc = jnp.clip(t_k, 0, tiles - 1)
    p_k = t_kc % ctx_size
    same_head = (t_kc // ctx_size) == (t_q // ctx_size)
    meet = (seg_lo[p_q] <= seg_hi[p_k]) & (seg_lo[p_k] <= seg_hi[p_q])
    need = (valid & same_head & meet).astype(jnp.int32).reshape(-1)
    kt = (jj + oo + REACH).astype(jnp.int32).reshape(-1)
    qp = p_q[:, 0].astype(jnp.int32)
    kp = p_k.astype(jnp.int32).reshape(-1)

    attended = flash(
        need, qp, kt, kp,
        own[0], kv_all[0], kv_all[1],
        seg_blocks.reshape(ctx_size, row_count, 1),
        seg_blocks.reshape(ctx_size, 1, row_count),
        score_scale,
    )

    slot_count = row_count // ctx_size
    dest_blocks = dest_all.reshape(ctx_size, row_count)
    dest_mine = dest_blocks[qp]
    place = (dest_mine // row_count) * slot_count + dest_mine % slot_count
    placed = jnp.zeros_like(attended).at[jj, place].set(attended)
    placed = placed.reshape(slots, ctx_size, slot_count, HD).transpose(1, 0, 2, 3)
    got = lax.all_to_all(placed, "ctx", split_axis=0, concat_axis=0, tiled=True)
    got = got.reshape(head_count, ctx_size, slot_count, HD).transpose(1, 2, 0, 3)
    owned_attended = got.reshape(row_count, row_width)

    owned_video_all = jnp.zeros_like(seg_all).at[dest_all].set(seg_all)
    owned_video = lax.dynamic_slice_in_dim(owned_video_all, me * row_count, row_count)

    head_terms = jnp.dot(owned_attended, out_weight, preferred_element_type=jnp.float32)
    mixed_rows = lax.psum_scatter(
        head_terms.astype(jnp.bfloat16), "head", scatter_dimension=1, tiled=True
    ).astype(jnp.float32)
    video_gates = jnp.dot(
        jax.nn.one_hot(timestep, gate_table.shape[0], dtype=jnp.float32),
        gate_table,
        precision=lax.Precision.HIGHEST,
    )
    token_gates = jnp.dot(
        jax.nn.one_hot(owned_video, timestep.shape[0], dtype=jnp.float32),
        video_gates,
        precision=lax.Precision.HIGHEST,
    )
    return (mixed_rows * token_gates).astype(jnp.bfloat16)


def solution(mesh):
    placed = (
        P(("batch", "ctx"), "head"),
        P(("batch", "ctx"), "head"),
        P(("batch", "ctx"), "head"),
        P("head"),
        P("head"),
        P(("batch", "ctx")),
        P(("batch", "ctx")),
        P("batch"),
        P("head", None),
        P(None, "head"),
    )
    return jax.shard_map(
        local, mesh=mesh, in_specs=placed, out_specs=P(("batch", "ctx"), "head"), check_vma=False
    )
```

```python
import functools
import math

import jax
import jax.numpy as jnp
from jax import lax
from jax.experimental import pallas as pl
from jax.experimental.pallas import tpu as pltpu
from jax.sharding import PartitionSpec as P

HD = 128
REACH = 4


def flash_kernel(
    need_ref, qp_ref, kt_ref, kp_ref,
    q_ref, k_ref, v_ref, qs_ref, ks_ref,
    o_ref, m_scr, l_scr, acc_scr, *, offsets, score_scale
):
    j = pl.program_id(0)
    o = pl.program_id(1)

    @pl.when(o == 0)
    def _():
        m_scr[...] = jnp.full_like(m_scr, -1e30)
        l_scr[...] = jnp.zeros_like(l_scr)
        acc_scr[...] = jnp.zeros_like(acc_scr)

    @pl.when(need_ref[j * offsets + o] != 0)
    def _():
        q = q_ref[0]
        k = k_ref[0]
        s = lax.dot_general(
            q, k, (((1,), (1,)), ((), ())), preferred_element_type=jnp.float32
        ) * score_scale
        mask = qs_ref[0] == ks_ref[0]
        s = jnp.where(mask, s, -1e30)
        m_prev = m_scr[...]
        m_new = jnp.maximum(m_prev, jnp.max(s, axis=1, keepdims=True))
        alpha = jnp.exp(m_prev - m_new)
        p = jnp.where(mask, jnp.exp(s - m_new), 0.0)
        l_scr[...] = alpha * l_scr[...] + jnp.sum(p, axis=1, keepdims=True)
        acc_scr[...] = alpha * acc_scr[...] + jnp.dot(
            p.astype(jnp.bfloat16), v_ref[0], preferred_element_type=jnp.float32
        )
        m_scr[...] = m_new

    @pl.when(o == offsets - 1)
    def _():
        o_ref[0] = (acc_scr[...] / l_scr[...]).astype(o_ref.dtype)


def flash(need, qp, kt, kp, q_tiles, k_tiles, v_tiles, seg_rows, seg_cols, score_scale):
    slots, rows, width = q_tiles.shape
    offsets = 2 * REACH + 1
    kern = functools.partial(flash_kernel, offsets=offsets, score_scale=score_scale)
    grid_spec = pltpu.PrefetchScalarGridSpec(
        num_scalar_prefetch=4,
        grid=(slots, offsets),
        in_specs=[
            pl.BlockSpec((1, rows, width), lambda j, o, nd, qp, kt, kp: (j, 0, 0)),
            pl.BlockSpec((1, rows, width), lambda j, o, nd, qp, kt, kp: (kt[j * offsets + o], 0, 0)),
            pl.BlockSpec((1, rows, width), lambda j, o, nd, qp, kt, kp: (kt[j * offsets + o], 0, 0)),
            pl.BlockSpec((1, rows, 1), lambda j, o, nd, qp, kt, kp: (qp[j], 0, 0)),
            pl.BlockSpec((1, 1, rows), lambda j, o, nd, qp, kt, kp: (kp[j * offsets + o], 0, 0)),
        ],
        out_specs=pl.BlockSpec((1, rows, width), lambda j, o, nd, qp, kt, kp: (j, 0, 0)),
        scratch_shapes=[
            pltpu.VMEM((rows, 1), jnp.float32),
            pltpu.VMEM((rows, 1), jnp.float32),
            pltpu.VMEM((rows, width), jnp.float32),
        ],
    )
    return pl.pallas_call(
        kern,
        grid_spec=grid_spec,
        out_shape=jax.ShapeDtypeStruct((slots, rows, width), jnp.bfloat16),
        compiler_params=pltpu.CompilerParams(
            dimension_semantics=("arbitrary", "arbitrary")
        ),
    )(need, qp, kt, kp, q_tiles, k_tiles, v_tiles, seg_rows, seg_cols)


def doubling_gather(piece, me, size):
    held = piece[None]
    shift = 1
    while shift < size:
        came = lax.ppermute(held, "ctx", [(e, (e + shift) % size) for e in range(size)])
        held = jnp.concatenate([came, held], axis=0)
        shift *= 2
    return jnp.roll(held, me + 1, axis=0)


def local(
    query_raw,
    key_raw,
    value_rows,
    query_gain,
    key_gain,
    segment,
    destination,
    timestep,
    out_weight,
    gate_table,
):
    row_count = query_raw.shape[0]
    row_width = query_raw.shape[1]
    head_count = row_width // HD
    ctx_size = lax.axis_size("ctx")
    total_width = row_width * lax.axis_size("head")
    score_scale = 1.0 / math.sqrt(HD)
    me = lax.axis_index("ctx")
    tiles = head_count * ctx_size
    slots = tiles // ctx_size

    marks = doubling_gather(jnp.stack([segment, destination]), me, ctx_size)
    seg_blocks = marks[:, 0]
    dest_blocks = marks[:, 1]
    query_float = query_raw.astype(jnp.float32)
    key_float = key_raw.astype(jnp.float32)
    query_sum, key_sum = lax.psum(
        (jnp.sum(query_float * query_float, axis=1), jnp.sum(key_float * key_float, axis=1)), "head"
    )
    queries = (
        query_float * lax.rsqrt(query_sum / total_width + 1e-06)[:, None] * query_gain
    ).astype(jnp.bfloat16)
    normed_keys = (key_float * lax.rsqrt(key_sum / total_width + 1e-06)[:, None] * key_gain).astype(
        jnp.bfloat16
    )

    qkv = jnp.stack([queries, normed_keys, value_rows]).reshape(3, row_count, head_count, HD)
    qkv = jnp.transpose(qkv, (0, 2, 1, 3))

    inverse = pow(slots, -1, ctx_size)
    own = []
    for j in range(slots):
        target = lax.rem(inverse * (me - j + ctx_size), ctx_size)
        head = (slots * target + j) // ctx_size
        piece = lax.dynamic_index_in_dim(qkv, head, axis=1, keepdims=False)
        perm = [((slots * e + j) % ctx_size, e) for e in range(ctx_size)]
        own.append(lax.ppermute(piece, "ctx", perm))
    own = jnp.stack(own, axis=1)

    kv_own = own[1:]
    left = lax.ppermute(
        kv_own[:, slots - REACH:], "ctx", [(e, e + 1) for e in range(ctx_size - 1)]
    )
    right = lax.ppermute(
        kv_own[:, :REACH], "ctx", [(e, e - 1) for e in range(1, ctx_size)]
    )
    kv_all = jnp.concatenate([left, kv_own, right], axis=1)

    seg_lo = seg_blocks[:, 0]
    seg_hi = seg_blocks[:, -1]

    offsets = 2 * REACH + 1
    jj = jnp.arange(slots, dtype=jnp.int32)[:, None]
    oo = jnp.arange(offsets, dtype=jnp.int32)[None, :] - REACH
    t_q = slots * me + jj
    t_k = t_q + oo
    p_q = t_q % ctx_size
    valid = (t_k >= 0) & (t_k < tiles)
    t_kc = jnp.clip(t_k, 0, tiles - 1)
    p_k = t_kc % ctx_size
    same_head = (t_kc // ctx_size) == (t_q // ctx_size)
    meet = (seg_lo[p_q] <= seg_hi[p_k]) & (seg_lo[p_k] <= seg_hi[p_q])
    need = (valid & same_head & meet).astype(jnp.int32).reshape(-1)
    kt = (jj + oo + REACH).astype(jnp.int32).reshape(-1)
    qp = p_q[:, 0].astype(jnp.int32)
    kp = p_k.astype(jnp.int32).reshape(-1)

    attended = flash(
        need, qp, kt, kp,
        own[0], kv_all[0], kv_all[1],
        seg_blocks.reshape(ctx_size, row_count, 1),
        seg_blocks.reshape(ctx_size, 1, row_count),
        score_scale,
    )

    slot_count = row_count // ctx_size
    dest_mine = dest_blocks[qp]
    place = (dest_mine // row_count) * slot_count + dest_mine % slot_count
    chooser = (
        place[:, None, :] == jnp.arange(row_count, dtype=jnp.int32)[None, :, None]
    ).astype(jnp.bfloat16)
    placed = jnp.einsum(
        "jsr,jrd->jsd", chooser, attended, preferred_element_type=jnp.float32
    ).astype(jnp.bfloat16)
    placed = placed.reshape(slots, ctx_size, slot_count, HD).transpose(1, 0, 2, 3)
    got = lax.all_to_all(placed, "ctx", split_axis=0, concat_axis=0, tiled=True)
    got = got.reshape(head_count, ctx_size, slot_count, HD).transpose(1, 2, 0, 3)
    owned_attended = got.reshape(row_count, row_width)

    wanted = (
        me * row_count
        + jnp.arange(ctx_size, dtype=jnp.int32)[:, None, None] * slot_count
        + jnp.arange(slot_count, dtype=jnp.int32)[None, :, None]
    )
    owned_video = jnp.sum(
        jnp.where(dest_blocks[:, None, :] == wanted, seg_blocks[:, None, :], 0), axis=2
    ).reshape(row_count)

    head_terms = jnp.dot(owned_attended, out_weight, preferred_element_type=jnp.float32)
    mixed_rows = lax.psum_scatter(
        head_terms.astype(jnp.bfloat16), "head", scatter_dimension=1, tiled=True
    ).astype(jnp.float32)
    video_gates = jnp.dot(
        jax.nn.one_hot(timestep, gate_table.shape[0], dtype=jnp.float32),
        gate_table,
        precision=lax.Precision.HIGHEST,
    )
    token_gates = jnp.dot(
        jax.nn.one_hot(owned_video, timestep.shape[0], dtype=jnp.float32),
        video_gates,
        precision=lax.Precision.HIGHEST,
    )
    return (mixed_rows * token_gates).astype(jnp.bfloat16)


def solution(mesh):
    placed = (
        P(("batch", "ctx"), "head"),
        P(("batch", "ctx"), "head"),
        P(("batch", "ctx"), "head"),
        P("head"),
        P("head"),
        P(("batch", "ctx")),
        P(("batch", "ctx")),
        P("batch"),
        P("head", None),
        P(None, "head"),
    )
    return jax.shard_map(
        local, mesh=mesh, in_specs=placed, out_specs=P(("batch", "ctx"), "head"), check_vma=False
    )
```

```python
import functools
import math

import jax
import jax.numpy as jnp
from jax import lax
from jax.experimental import pallas as pl
from jax.experimental.pallas import tpu as pltpu
from jax.sharding import PartitionSpec as P

HD = 128
REACH = 4


def flash_kernel(
    need_ref, qp_ref, kt_ref, kp_ref,
    q_ref, k_ref, v_ref, qs_ref, ks_ref, m_in, l_in, acc_in,
    *refs, offsets, score_scale, last
):
    if last:
        o_ref, m_scr, l_scr, acc_scr = refs
    else:
        m_scr, l_scr, acc_scr = refs
    j = pl.program_id(0)
    o = pl.program_id(1)

    @pl.when(o == 0)
    def _():
        m_scr[0] = m_in[0]
        l_scr[0] = l_in[0]
        acc_scr[0] = acc_in[0]

    @pl.when(need_ref[j * offsets + o] != 0)
    def _():
        q = q_ref[0]
        k = k_ref[0]
        s = lax.dot_general(
            q, k, (((1,), (1,)), ((), ())), preferred_element_type=jnp.float32
        ) * score_scale
        mask = qs_ref[0] == ks_ref[0]
        s = jnp.where(mask, s, -1e30)
        m_prev = m_scr[0]
        m_new = jnp.maximum(m_prev, jnp.max(s, axis=1, keepdims=True))
        alpha = jnp.exp(m_prev - m_new)
        p = jnp.where(mask, jnp.exp(s - m_new), 0.0)
        l_scr[0] = alpha * l_scr[0] + jnp.sum(p, axis=1, keepdims=True)
        acc_scr[0] = alpha * acc_scr[0] + jnp.dot(
            p.astype(jnp.bfloat16), v_ref[0], preferred_element_type=jnp.float32
        )
        m_scr[0] = m_new

    if last:
        @pl.when(o == offsets - 1)
        def _():
            o_ref[0] = (acc_scr[0] / l_scr[0]).astype(o_ref.dtype)


def flash(need, qp, kt, kp, q_tiles, k_tiles, v_tiles, seg_rows, seg_cols, carry, score_scale, last, work):
    slots, rows, width = q_tiles.shape
    offsets = 2 * REACH + 1
    kern = functools.partial(flash_kernel, offsets=offsets, score_scale=score_scale, last=last)
    tile = pl.BlockSpec((1, rows, width), lambda j, o, nd, qp, kt, kp: (j, 0, 0))
    column = pl.BlockSpec((1, rows, 1), lambda j, o, nd, qp, kt, kp: (j, 0, 0))
    carry_specs = [column, column, tile]
    carry_shapes = [
        jax.ShapeDtypeStruct((slots, rows, 1), jnp.float32),
        jax.ShapeDtypeStruct((slots, rows, 1), jnp.float32),
        jax.ShapeDtypeStruct((slots, rows, width), jnp.float32),
    ]
    if last:
        out_specs = tile
        out_shape = jax.ShapeDtypeStruct((slots, rows, width), jnp.bfloat16)
        scratch = [
            pltpu.VMEM((1, rows, 1), jnp.float32),
            pltpu.VMEM((1, rows, 1), jnp.float32),
            pltpu.VMEM((1, rows, width), jnp.float32),
        ]
    else:
        out_specs = carry_specs
        out_shape = carry_shapes
        scratch = []
    grid_spec = pltpu.PrefetchScalarGridSpec(
        num_scalar_prefetch=4,
        grid=(slots, offsets),
        in_specs=[
            tile,
            pl.BlockSpec((1, rows, width), lambda j, o, nd, qp, kt, kp: (kt[j * offsets + o], 0, 0)),
            pl.BlockSpec((1, rows, width), lambda j, o, nd, qp, kt, kp: (kt[j * offsets + o], 0, 0)),
            pl.BlockSpec((1, rows, 1), lambda j, o, nd, qp, kt, kp: (qp[j], 0, 0)),
            pl.BlockSpec((1, 1, rows), lambda j, o, nd, qp, kt, kp: (kp[j * offsets + o], 0, 0)),
        ] + carry_specs,
        out_specs=out_specs,
        scratch_shapes=scratch,
    )
    return pl.pallas_call(
        kern,
        grid_spec=grid_spec,
        out_shape=out_shape,
        compiler_params=pltpu.CompilerParams(
            dimension_semantics=("arbitrary", "arbitrary")
        ),
        cost_estimate=pl.CostEstimate(
            flops=work * rows * rows * width * 4,
            transcendentals=work * rows * rows,
            bytes_accessed=work * rows * width * 4,
        ),
    )(need, qp, kt, kp, q_tiles, k_tiles, v_tiles, seg_rows, seg_cols, *carry)


def doubling_gather(piece, me, size):
    held = piece[None]
    shift = 1
    while shift < size:
        came = lax.ppermute(held, "ctx", [(e, (e + shift) % size) for e in range(size)])
        held = jnp.concatenate([came, held], axis=0)
        shift *= 2
    return jnp.roll(held, me + 1, axis=0)


def local(
    query_raw,
    key_raw,
    value_rows,
    query_gain,
    key_gain,
    segment,
    destination,
    timestep,
    out_weight,
    gate_table,
):
    row_count = query_raw.shape[0]
    row_width = query_raw.shape[1]
    head_count = row_width // HD
    ctx_size = lax.axis_size("ctx")
    total_width = row_width * lax.axis_size("head")
    score_scale = 1.0 / math.sqrt(HD)
    me = lax.axis_index("ctx")
    tiles = head_count * ctx_size
    slots = tiles // ctx_size

    marks = doubling_gather(jnp.stack([segment, destination]), me, ctx_size)
    seg_blocks = marks[:, 0]
    dest_blocks = marks[:, 1]
    query_float = query_raw.astype(jnp.float32)
    key_float = key_raw.astype(jnp.float32)
    query_sum, key_sum = lax.psum(
        (jnp.sum(query_float * query_float, axis=1), jnp.sum(key_float * key_float, axis=1)), "head"
    )
    queries = (
        query_float * lax.rsqrt(query_sum / total_width + 1e-06)[:, None] * query_gain
    ).astype(jnp.bfloat16)
    normed_keys = (key_float * lax.rsqrt(key_sum / total_width + 1e-06)[:, None] * key_gain).astype(
        jnp.bfloat16
    )

    qkv = jnp.stack([queries, normed_keys, value_rows]).reshape(3, row_count, head_count, HD)
    qkv = jnp.transpose(qkv, (0, 2, 1, 3))

    inverse = pow(slots, -1, ctx_size)
    own = []
    for j in range(slots):
        target = lax.rem(inverse * (me - j + ctx_size), ctx_size)
        head = (slots * target + j) // ctx_size
        piece = lax.dynamic_index_in_dim(qkv, head, axis=1, keepdims=False)
        perm = [((slots * e + j) % ctx_size, e) for e in range(ctx_size)]
        own.append(lax.ppermute(piece, "ctx", perm))
    own = jnp.stack(own, axis=1)

    kv_own = own[1:]
    left = lax.ppermute(
        kv_own[:, slots - REACH:], "ctx", [(e, e + 1) for e in range(ctx_size - 1)]
    )
    right = lax.ppermute(
        kv_own[:, :REACH], "ctx", [(e, e - 1) for e in range(1, ctx_size)]
    )
    kv_all = jnp.concatenate([left, kv_own, right], axis=1)

    seg_lo = seg_blocks[:, 0]
    seg_hi = seg_blocks[:, -1]

    offsets = 2 * REACH + 1
    jj = jnp.arange(slots, dtype=jnp.int32)[:, None]
    oo = jnp.arange(offsets, dtype=jnp.int32)[None, :] - REACH
    t_q = slots * me + jj
    t_k = t_q + oo
    p_q = t_q % ctx_size
    valid = (t_k >= 0) & (t_k < tiles)
    t_kc = jnp.clip(t_k, 0, tiles - 1)
    p_k = t_kc % ctx_size
    same_head = (t_kc // ctx_size) == (t_q // ctx_size)
    meet = (seg_lo[p_q] <= seg_hi[p_k]) & (seg_lo[p_k] <= seg_hi[p_q])
    kt = (jj + oo + REACH).astype(jnp.int32).reshape(-1)
    qp = p_q[:, 0].astype(jnp.int32)
    kp = p_k.astype(jnp.int32).reshape(-1)

    kt_own = jj + oo
    is_own = (kt_own >= 0) & (kt_own < slots)
    need_all = valid & same_head & meet
    need_own = (need_all & is_own).astype(jnp.int32).reshape(-1)
    need_far = (need_all & ~is_own).astype(jnp.int32).reshape(-1)
    kt_near = jnp.clip(kt_own, 0, slots - 1).astype(jnp.int32).reshape(-1)
    seg_rows = seg_blocks.reshape(ctx_size, row_count, 1)
    seg_cols = seg_blocks.reshape(ctx_size, 1, row_count)
    carry = (
        jnp.full((slots, row_count, 1), -1e30, jnp.float32),
        jnp.zeros((slots, row_count, 1), jnp.float32),
        jnp.zeros((slots, row_count, HD), jnp.float32),
    )
    carry = flash(
        need_own, qp, kt_near, kp, own[0], own[1], own[2], seg_rows, seg_cols, carry,
        score_scale, False, 15,
    )
    attended = flash(
        need_far, qp, kt, kp, own[0], kv_all[0], kv_all[1], seg_rows, seg_cols, carry,
        score_scale, True, 15,
    )

    slot_count = row_count // ctx_size
    dest_mine = dest_blocks[qp]
    place = (dest_mine // row_count) * slot_count + dest_mine % slot_count
    chooser = (
        place[:, None, :] == jnp.arange(row_count, dtype=jnp.int32)[None, :, None]
    ).astype(jnp.bfloat16)
    placed = jnp.einsum(
        "jsr,jrd->jsd", chooser, attended, preferred_element_type=jnp.float32
    ).astype(jnp.bfloat16)
    placed = placed.reshape(slots, ctx_size, slot_count, HD).transpose(1, 0, 2, 3)

    wanted = (
        me * row_count
        + jnp.arange(ctx_size, dtype=jnp.int32)[:, None, None] * slot_count
        + jnp.arange(slot_count, dtype=jnp.int32)[None, :, None]
    )
    owned_video = jnp.sum(
        jnp.where(dest_blocks[:, None, :] == wanted, seg_blocks[:, None, :], 0), axis=2
    )
    video_gates = jnp.dot(
        jax.nn.one_hot(timestep, gate_table.shape[0], dtype=jnp.float32),
        gate_table,
        precision=lax.Precision.HIGHEST,
    )
    halves = 2
    part = slot_count // halves
    results = []
    for half in range(halves):
        piece = placed[:, :, half * part:(half + 1) * part]
        got = lax.all_to_all(piece, "ctx", split_axis=0, concat_axis=0, tiled=True)
        got = got.reshape(head_count, ctx_size, part, HD).transpose(1, 2, 0, 3)
        owned_attended = got.reshape(ctx_size * part, row_width)
        head_terms = jnp.dot(owned_attended, out_weight, preferred_element_type=jnp.float32)
        mixed_rows = lax.psum_scatter(
            head_terms.astype(jnp.bfloat16), "head", scatter_dimension=1, tiled=True
        ).astype(jnp.float32)
        videos = owned_video[:, half * part:(half + 1) * part].reshape(-1)
        token_gates = jnp.dot(
            jax.nn.one_hot(videos, timestep.shape[0], dtype=jnp.float32),
            video_gates,
            precision=lax.Precision.HIGHEST,
        )
        gated = (mixed_rows * token_gates).astype(jnp.bfloat16)
        results.append(gated.reshape(ctx_size, part, -1))
    return jnp.concatenate(results, axis=1).reshape(row_count, -1)


def solution(mesh):
    placed = (
        P(("batch", "ctx"), "head"),
        P(("batch", "ctx"), "head"),
        P(("batch", "ctx"), "head"),
        P("head"),
        P("head"),
        P(("batch", "ctx")),
        P(("batch", "ctx")),
        P("batch"),
        P("head", None),
        P(None, "head"),
    )
    return jax.shard_map(
        local, mesh=mesh, in_specs=placed, out_specs=P(("batch", "ctx"), "head"), check_vma=False
    )
```

```python
import functools
import math

import jax
import jax.numpy as jnp
from jax import lax
from jax.experimental import pallas as pl
from jax.experimental.pallas import tpu as pltpu
from jax.sharding import PartitionSpec as P

HD = 128
REACH = 4


def flash_kernel(
    need_ref, qp_ref, kt_ref, kp_ref,
    q_ref, k_ref, v_ref, qs_ref, ks_ref,
    o_ref, m_scr, l_scr, acc_scr, *, offsets, score_scale
):
    j = pl.program_id(0)
    o = pl.program_id(1)

    @pl.when(o == 0)
    def _():
        m_scr[...] = jnp.full_like(m_scr, -1e30)
        l_scr[...] = jnp.zeros_like(l_scr)
        acc_scr[...] = jnp.zeros_like(acc_scr)

    @pl.when(need_ref[j * offsets + o] != 0)
    def _():
        q = q_ref[0]
        k = k_ref[0]
        s = lax.dot_general(
            q, k, (((1,), (1,)), ((), ())), preferred_element_type=jnp.float32
        ) * score_scale
        mask = qs_ref[0] == ks_ref[0]
        s = jnp.where(mask, s, -1e30)
        m_prev = m_scr[...]
        m_new = jnp.maximum(m_prev, jnp.max(s, axis=1, keepdims=True))
        alpha = jnp.exp(m_prev - m_new)
        p = jnp.where(mask, jnp.exp(s - m_new), 0.0)
        l_scr[...] = alpha * l_scr[...] + jnp.sum(p, axis=1, keepdims=True)
        acc_scr[...] = alpha * acc_scr[...] + jnp.dot(
            p.astype(jnp.bfloat16), v_ref[0], preferred_element_type=jnp.float32
        )
        m_scr[...] = m_new

    @pl.when(o == offsets - 1)
    def _():
        o_ref[0] = (acc_scr[...] / l_scr[...]).astype(o_ref.dtype)


def flash(need, qp, kt, kp, q_tiles, k_tiles, v_tiles, seg_rows, seg_cols, score_scale):
    slots, rows, width = q_tiles.shape
    offsets = 2 * REACH + 1
    kern = functools.partial(flash_kernel, offsets=offsets, score_scale=score_scale)
    grid_spec = pltpu.PrefetchScalarGridSpec(
        num_scalar_prefetch=4,
        grid=(slots, offsets),
        in_specs=[
            pl.BlockSpec((1, rows, width), lambda j, o, nd, qp, kt, kp: (j, 0, 0)),
            pl.BlockSpec((1, rows, width), lambda j, o, nd, qp, kt, kp: (kt[j * offsets + o], 0, 0)),
            pl.BlockSpec((1, rows, width), lambda j, o, nd, qp, kt, kp: (kt[j * offsets + o], 0, 0)),
            pl.BlockSpec((1, rows, 1), lambda j, o, nd, qp, kt, kp: (qp[j], 0, 0)),
            pl.BlockSpec((1, 1, rows), lambda j, o, nd, qp, kt, kp: (kp[j * offsets + o], 0, 0)),
        ],
        out_specs=pl.BlockSpec((1, rows, width), lambda j, o, nd, qp, kt, kp: (j, 0, 0)),
        scratch_shapes=[
            pltpu.VMEM((rows, 1), jnp.float32),
            pltpu.VMEM((rows, 1), jnp.float32),
            pltpu.VMEM((rows, width), jnp.float32),
        ],
    )
    return pl.pallas_call(
        kern,
        grid_spec=grid_spec,
        out_shape=jax.ShapeDtypeStruct((slots, rows, width), jnp.bfloat16),
        compiler_params=pltpu.CompilerParams(
            dimension_semantics=("arbitrary", "arbitrary")
        ),
    )(need, qp, kt, kp, q_tiles, k_tiles, v_tiles, seg_rows, seg_cols)


def local(
    query_raw,
    key_raw,
    value_rows,
    query_gain,
    key_gain,
    segment,
    destination,
    timestep,
    out_weight,
    gate_table,
):
    row_count = query_raw.shape[0]
    row_width = query_raw.shape[1]
    head_count = row_width // HD
    ctx_size = lax.axis_size("ctx")
    total_width = row_width * lax.axis_size("head")
    score_scale = 1.0 / math.sqrt(HD)
    me = lax.axis_index("ctx")
    tiles = head_count * ctx_size
    slots = tiles // ctx_size

    query_float = query_raw.astype(jnp.float32)
    key_float = key_raw.astype(jnp.float32)
    query_sum, key_sum = lax.psum(
        (jnp.sum(query_float * query_float, axis=1), jnp.sum(key_float * key_float, axis=1)), "head"
    )
    queries = (
        query_float * lax.rsqrt(query_sum / total_width + 1e-06)[:, None] * query_gain
    ).astype(jnp.bfloat16)
    normed_keys = (key_float * lax.rsqrt(key_sum / total_width + 1e-06)[:, None] * key_gain).astype(
        jnp.bfloat16
    )

    qkv = jnp.stack([queries, normed_keys, value_rows]).reshape(3, row_count, head_count, HD)
    qkv = jnp.transpose(qkv, (0, 2, 1, 3))
    meta = jnp.stack([segment, destination // 64, destination % 64]).astype(jnp.bfloat16)
    meta = meta.reshape(-1, HD)
    body_rows = 3 * row_count
    pad = (-(body_rows + meta.shape[0])) % 16

    inverse = pow(slots, -1, ctx_size)
    own = []
    own_meta = []
    for j in range(slots):
        target = lax.rem(inverse * (me - j + ctx_size), ctx_size)
        head = (slots * target + j) // ctx_size
        piece = lax.dynamic_index_in_dim(qkv, head, axis=1, keepdims=False)
        piece = jnp.concatenate(
            [piece.reshape(body_rows, HD), meta, jnp.zeros((pad, HD), jnp.bfloat16)], axis=0
        )
        perm = [((slots * e + j) % ctx_size, e) for e in range(ctx_size)]
        came = lax.ppermute(piece, "ctx", perm)
        own.append(came[:body_rows].reshape(3, row_count, HD))
        own_meta.append(came[body_rows:body_rows + meta.shape[0]].reshape(3, row_count))
    own = jnp.stack(own, axis=1)
    own_meta = jnp.stack(own_meta, axis=1).astype(jnp.int32)
    seg_own = own_meta[0]
    dest_own = own_meta[1] * 64 + own_meta[2]

    kv_own = own[1:]
    seg_own_b = seg_own.astype(jnp.bfloat16).reshape(slots, row_count // HD, HD)
    halo_rows = 2 * REACH * row_count

    def halo(kv_part, seg_part):
        return jnp.concatenate(
            [kv_part.reshape(halo_rows, HD), seg_part.reshape(REACH * row_count // HD, HD)], axis=0
        )

    left = lax.ppermute(
        halo(kv_own[:, slots - REACH:], seg_own_b[slots - REACH:]),
        "ctx",
        [(e, e + 1) for e in range(ctx_size - 1)],
    )
    right = lax.ppermute(
        halo(kv_own[:, :REACH], seg_own_b[:REACH]),
        "ctx",
        [(e, e - 1) for e in range(1, ctx_size)],
    )

    def unpack(got):
        kv_part = got[:halo_rows].reshape(2, REACH, row_count, HD)
        seg_part = got[halo_rows:].reshape(REACH, row_count).astype(jnp.int32)
        return kv_part, seg_part

    left_kv, left_seg = unpack(left)
    right_kv, right_seg = unpack(right)
    kv_all = jnp.concatenate([left_kv, kv_own, right_kv], axis=1)
    seg_keys = jnp.concatenate([left_seg, seg_own, right_seg], axis=0)
    seg_lo = seg_keys[:, 0]
    seg_hi = seg_keys[:, -1]

    offsets = 2 * REACH + 1
    jj = jnp.arange(slots, dtype=jnp.int32)[:, None]
    oo = jnp.arange(offsets, dtype=jnp.int32)[None, :] - REACH
    t_q = slots * me + jj
    t_k = t_q + oo
    valid = (t_k >= 0) & (t_k < tiles)
    t_kc = jnp.clip(t_k, 0, tiles - 1)
    same_head = (t_kc // ctx_size) == (t_q // ctx_size)
    q_index = jj + REACH
    k_index = jj + oo + REACH
    meet = (seg_lo[q_index] <= seg_hi[k_index]) & (seg_lo[k_index] <= seg_hi[q_index])
    need_b = (valid & same_head & meet).reshape(-1)
    need = need_b.astype(jnp.int32)
    steps = jnp.arange(need.shape[0], dtype=jnp.int32)
    latest = lax.cummax(jnp.where(need_b, steps, -1), axis=0)
    source = jnp.where(latest < 0, jnp.argmax(need_b).astype(jnp.int32), latest)
    kt = k_index.astype(jnp.int32).reshape(-1)[source]
    qp = q_index[:, 0].astype(jnp.int32)
    kp = kt

    attended = flash(
        need, qp, kt, kp,
        own[0], kv_all[0], kv_all[1],
        seg_keys.reshape(-1, row_count, 1),
        seg_keys.reshape(-1, 1, row_count),
        score_scale,
    )

    slot_count = row_count // ctx_size
    place = (dest_own // row_count) * slot_count + dest_own % slot_count
    chooser = (
        place[:, None, :] == jnp.arange(row_count, dtype=jnp.int32)[None, :, None]
    ).astype(jnp.bfloat16)
    placed = jnp.einsum(
        "jsr,jrd->jsd", chooser, attended, preferred_element_type=jnp.float32
    ).astype(jnp.bfloat16)
    placed_seg = jnp.einsum(
        "jsr,jr->js", chooser, seg_own.astype(jnp.bfloat16), preferred_element_type=jnp.float32
    ).astype(jnp.bfloat16)
    placed = placed.reshape(slots, ctx_size, slot_count, HD).transpose(1, 0, 2, 3)
    placed = placed.reshape(ctx_size, slots * slot_count, HD)
    placed_seg = placed_seg.reshape(slots, ctx_size, slot_count).transpose(1, 0, 2)
    seg_width = slots * slot_count
    seg_rows_n = -(-seg_width // HD)
    placed_seg = jnp.pad(
        placed_seg.reshape(ctx_size, seg_width), ((0, 0), (0, seg_rows_n * HD - seg_width))
    ).reshape(ctx_size, seg_rows_n, HD)
    extra = (-(seg_width + seg_rows_n)) % 16
    payload = jnp.concatenate(
        [placed, placed_seg, jnp.zeros((ctx_size, extra, HD), jnp.bfloat16)], axis=1
    )
    got = lax.all_to_all(payload, "ctx", split_axis=0, concat_axis=0, tiled=True)
    got_att = got[:, :seg_width].reshape(tiles, slot_count, HD)
    got_att = got_att.reshape(head_count, ctx_size, slot_count, HD).transpose(1, 2, 0, 3)
    owned_attended = got_att.reshape(row_count, row_width)
    got_seg = got[:, seg_width:seg_width + seg_rows_n].reshape(ctx_size, seg_rows_n * HD)
    got_seg = got_seg[:, :seg_width].reshape(tiles, slot_count)
    owned_video = got_seg[:ctx_size].reshape(row_count).astype(jnp.int32)

    head_terms = jnp.dot(owned_attended, out_weight, preferred_element_type=jnp.float32)
    mixed_rows = lax.psum_scatter(
        head_terms.astype(jnp.bfloat16), "head", scatter_dimension=1, tiled=True
    ).astype(jnp.float32)
    video_gates = jnp.dot(
        jax.nn.one_hot(timestep, gate_table.shape[0], dtype=jnp.float32),
        gate_table,
        precision=lax.Precision.HIGHEST,
    )
    token_gates = jnp.dot(
        jax.nn.one_hot(owned_video, timestep.shape[0], dtype=jnp.float32),
        video_gates,
        precision=lax.Precision.HIGHEST,
    )
    return (mixed_rows * token_gates).astype(jnp.bfloat16)


def solution(mesh):
    placed = (
        P(("batch", "ctx"), "head"),
        P(("batch", "ctx"), "head"),
        P(("batch", "ctx"), "head"),
        P("head"),
        P("head"),
        P(("batch", "ctx")),
        P(("batch", "ctx")),
        P("batch"),
        P("head", None),
        P(None, "head"),
    )
    return jax.shard_map(
        local, mesh=mesh, in_specs=placed, out_specs=P(("batch", "ctx"), "head"), check_vma=False
    )
```

```python
import functools
import math

import jax
import jax.numpy as jnp
from jax import lax
from jax.experimental import pallas as pl
from jax.experimental.pallas import tpu as pltpu
from jax.sharding import PartitionSpec as P

HD = 128
REACH = 4


def flash_kernel(
    need_ref, qp_ref, kt_ref, kp_ref,
    q_ref, k_ref, v_ref, qs_ref, ks_ref,
    o_ref, m_scr, l_scr, acc_scr, *, offsets, score_scale
):
    j = pl.program_id(0)
    o = pl.program_id(1)

    @pl.when(o == 0)
    def _():
        m_scr[...] = jnp.full_like(m_scr, -1e30)
        l_scr[...] = jnp.zeros_like(l_scr)
        acc_scr[...] = jnp.zeros_like(acc_scr)

    @pl.when(need_ref[j * offsets + o] != 0)
    def _():
        q = q_ref[0]
        k = k_ref[0]
        s = lax.dot_general(
            q, k, (((1,), (1,)), ((), ())), preferred_element_type=jnp.float32
        ) * score_scale
        mask = qs_ref[0] == ks_ref[0]
        s = jnp.where(mask, s, -1e30)
        m_prev = m_scr[...]
        m_new = jnp.maximum(m_prev, jnp.max(s, axis=1, keepdims=True))
        alpha = jnp.exp(m_prev - m_new)
        p = jnp.where(mask, jnp.exp(s - m_new), 0.0)
        l_scr[...] = alpha * l_scr[...] + jnp.sum(p, axis=1, keepdims=True)
        acc_scr[...] = alpha * acc_scr[...] + jnp.dot(
            p.astype(jnp.bfloat16), v_ref[0], preferred_element_type=jnp.float32
        )
        m_scr[...] = m_new

    @pl.when(o == offsets - 1)
    def _():
        o_ref[0] = (acc_scr[...] / l_scr[...]).astype(o_ref.dtype)


def flash(need, qp, kt, kp, q_tiles, k_tiles, v_tiles, seg_rows, seg_cols, score_scale):
    slots, rows, width = q_tiles.shape
    offsets = 2 * REACH + 1
    kern = functools.partial(flash_kernel, offsets=offsets, score_scale=score_scale)
    grid_spec = pltpu.PrefetchScalarGridSpec(
        num_scalar_prefetch=4,
        grid=(slots, offsets),
        in_specs=[
            pl.BlockSpec((1, rows, width), lambda j, o, nd, qp, kt, kp: (j, 0, 0)),
            pl.BlockSpec((1, rows, width), lambda j, o, nd, qp, kt, kp: (kt[j * offsets + o], 0, 0)),
            pl.BlockSpec((1, rows, width), lambda j, o, nd, qp, kt, kp: (kt[j * offsets + o], 0, 0)),
            pl.BlockSpec((1, rows, 1), lambda j, o, nd, qp, kt, kp: (qp[j], 0, 0)),
            pl.BlockSpec((1, 1, rows), lambda j, o, nd, qp, kt, kp: (kp[j * offsets + o], 0, 0)),
        ],
        out_specs=pl.BlockSpec((1, rows, width), lambda j, o, nd, qp, kt, kp: (j, 0, 0)),
        scratch_shapes=[
            pltpu.VMEM((rows, 1), jnp.float32),
            pltpu.VMEM((rows, 1), jnp.float32),
            pltpu.VMEM((rows, width), jnp.float32),
        ],
    )
    return pl.pallas_call(
        kern,
        grid_spec=grid_spec,
        out_shape=jax.ShapeDtypeStruct((slots, rows, width), jnp.bfloat16),
        compiler_params=pltpu.CompilerParams(
            dimension_semantics=("arbitrary", "arbitrary")
        ),
    )(need, qp, kt, kp, q_tiles, k_tiles, v_tiles, seg_rows, seg_cols)


def doubling_gather(piece, me, size):
    held = piece[None]
    shift = 1
    while shift < size:
        came = lax.ppermute(held, "ctx", [(e, (e + shift) % size) for e in range(size)])
        held = jnp.concatenate([came, held], axis=0)
        shift *= 2
    return jnp.roll(held, me + 1, axis=0)


def local(
    query_raw,
    key_raw,
    value_rows,
    query_gain,
    key_gain,
    segment,
    destination,
    timestep,
    out_weight,
    gate_table,
):
    row_count = query_raw.shape[0]
    row_width = query_raw.shape[1]
    head_count = row_width // HD
    ctx_size = lax.axis_size("ctx")
    total_width = row_width * lax.axis_size("head")
    score_scale = 1.0 / math.sqrt(HD)
    me = lax.axis_index("ctx")
    tiles = head_count * ctx_size
    slots = tiles // ctx_size

    marks = doubling_gather(jnp.stack([segment, destination]), me, ctx_size)
    seg_blocks = marks[:, 0]
    dest_blocks = marks[:, 1]
    query_float = query_raw.astype(jnp.float32)
    key_float = key_raw.astype(jnp.float32)
    query_sum, key_sum = lax.psum(
        (jnp.sum(query_float * query_float, axis=1), jnp.sum(key_float * key_float, axis=1)), "head"
    )
    queries = (
        query_float * lax.rsqrt(query_sum / total_width + 1e-06)[:, None] * query_gain
    ).astype(jnp.bfloat16)
    normed_keys = (key_float * lax.rsqrt(key_sum / total_width + 1e-06)[:, None] * key_gain).astype(
        jnp.bfloat16
    )

    qkv = jnp.stack([queries, normed_keys, value_rows]).reshape(3, row_count, head_count, HD)
    qkv = jnp.transpose(qkv, (0, 2, 1, 3))

    inverse = pow(slots, -1, ctx_size)
    own = []
    for j in range(slots):
        target = lax.rem(inverse * (me - j + ctx_size), ctx_size)
        head = (slots * target + j) // ctx_size
        piece = lax.dynamic_index_in_dim(qkv, head, axis=1, keepdims=False)
        perm = [((slots * e + j) % ctx_size, e) for e in range(ctx_size)]
        own.append(lax.ppermute(piece, "ctx", perm))
    own = jnp.stack(own, axis=1)

    kv_own = own[1:]
    left = lax.ppermute(
        kv_own[:, slots - REACH:], "ctx", [(e, e + 1) for e in range(ctx_size - 1)]
    )
    right = lax.ppermute(
        kv_own[:, :REACH], "ctx", [(e, e - 1) for e in range(1, ctx_size)]
    )
    kv_all = jnp.concatenate([left, kv_own, right], axis=1)

    seg_lo = seg_blocks[:, 0]
    seg_hi = seg_blocks[:, -1]

    offsets = 2 * REACH + 1
    jj = jnp.arange(slots, dtype=jnp.int32)[:, None]
    oo = jnp.arange(offsets, dtype=jnp.int32)[None, :] - REACH
    t_q = slots * me + jj
    t_k = t_q + oo
    p_q = t_q % ctx_size
    valid = (t_k >= 0) & (t_k < tiles)
    t_kc = jnp.clip(t_k, 0, tiles - 1)
    p_k = t_kc % ctx_size
    same_head = (t_kc // ctx_size) == (t_q // ctx_size)
    meet = (seg_lo[p_q] <= seg_hi[p_k]) & (seg_lo[p_k] <= seg_hi[p_q])
    need_b = (valid & same_head & meet).reshape(-1)
    need = need_b.astype(jnp.int32)
    steps = jnp.arange(need.shape[0], dtype=jnp.int32)
    latest = lax.cummax(jnp.where(need_b, steps, -1), axis=0)
    source = jnp.where(latest < 0, jnp.argmax(need_b).astype(jnp.int32), latest)
    kt = (jj + oo + REACH).astype(jnp.int32).reshape(-1)[source]
    qp = p_q[:, 0].astype(jnp.int32)
    kp = p_k.astype(jnp.int32).reshape(-1)[source]

    attended = flash(
        need, qp, kt, kp,
        own[0], kv_all[0], kv_all[1],
        seg_blocks.reshape(ctx_size, row_count, 1),
        seg_blocks.reshape(ctx_size, 1, row_count),
        score_scale,
    )

    slot_count = row_count // ctx_size
    dest_mine = dest_blocks[qp]
    place = (dest_mine // row_count) * slot_count + dest_mine % slot_count
    chooser = (
        place[:, None, :] == jnp.arange(row_count, dtype=jnp.int32)[None, :, None]
    ).astype(jnp.bfloat16)
    placed = jnp.einsum(
        "jsr,jrd->jsd", chooser, attended, preferred_element_type=jnp.float32
    ).astype(jnp.bfloat16)
    placed = placed.reshape(slots, ctx_size, slot_count, HD).transpose(1, 0, 2, 3)
    got = lax.all_to_all(placed, "ctx", split_axis=0, concat_axis=0, tiled=True)
    got = got.reshape(head_count, ctx_size, slot_count, HD).transpose(1, 2, 0, 3)
    owned_attended = got.reshape(row_count, row_width)

    wanted = (
        me * row_count
        + jnp.arange(ctx_size, dtype=jnp.int32)[:, None, None] * slot_count
        + jnp.arange(slot_count, dtype=jnp.int32)[None, :, None]
    )
    owned_video = jnp.sum(
        jnp.where(dest_blocks[:, None, :] == wanted, seg_blocks[:, None, :], 0), axis=2
    ).reshape(row_count)

    head_terms = jnp.dot(owned_attended, out_weight, preferred_element_type=jnp.float32)
    mixed_rows = lax.psum_scatter(
        head_terms.astype(jnp.bfloat16), "head", scatter_dimension=1, tiled=True
    ).astype(jnp.float32)
    video_gates = jnp.dot(
        jax.nn.one_hot(timestep, gate_table.shape[0], dtype=jnp.float32),
        gate_table,
        precision=lax.Precision.HIGHEST,
    )
    token_gates = jnp.dot(
        jax.nn.one_hot(owned_video, timestep.shape[0], dtype=jnp.float32),
        video_gates,
        precision=lax.Precision.HIGHEST,
    )
    return (mixed_rows * token_gates).astype(jnp.bfloat16)


def solution(mesh):
    placed = (
        P(("batch", "ctx"), "head"),
        P(("batch", "ctx"), "head"),
        P(("batch", "ctx"), "head"),
        P("head"),
        P("head"),
        P(("batch", "ctx")),
        P(("batch", "ctx")),
        P("batch"),
        P("head", None),
        P(None, "head"),
    )
    return jax.shard_map(
        local, mesh=mesh, in_specs=placed, out_specs=P(("batch", "ctx"), "head"), check_vma=False
    )
```

```python
import functools
import math

import jax
import jax.numpy as jnp
from jax import lax
from jax.experimental import pallas as pl
from jax.experimental.pallas import tpu as pltpu
from jax.sharding import PartitionSpec as P

HD = 128
REACH = 4


def flash_kernel(
    need_ref, qp_ref, kt_ref, kp_ref,
    q_ref, k_ref, v_ref, qs_ref, ks_ref,
    o_ref, m_scr, l_scr, acc_scr, *, offsets, score_scale
):
    j = pl.program_id(0)
    o = pl.program_id(1)

    @pl.when(o == 0)
    def _():
        m_scr[...] = jnp.full_like(m_scr, -1e30)
        l_scr[...] = jnp.zeros_like(l_scr)
        acc_scr[...] = jnp.zeros_like(acc_scr)

    @pl.when(need_ref[j * offsets + o] != 0)
    def _():
        q = q_ref[0]
        k = k_ref[0]
        s = lax.dot_general(
            q, k, (((1,), (1,)), ((), ())), preferred_element_type=jnp.float32
        ) * score_scale
        mask = qs_ref[0] == ks_ref[0]
        s = jnp.where(mask, s, -1e30)
        m_prev = m_scr[...]
        m_new = jnp.maximum(m_prev, jnp.max(s, axis=1, keepdims=True))
        alpha = jnp.exp(m_prev - m_new)
        p = jnp.where(mask, jnp.exp(s - m_new), 0.0)
        l_scr[...] = alpha * l_scr[...] + jnp.sum(p, axis=1, keepdims=True)
        acc_scr[...] = alpha * acc_scr[...] + jnp.dot(
            p.astype(jnp.bfloat16), v_ref[0], preferred_element_type=jnp.float32
        )
        m_scr[...] = m_new

    @pl.when(o == offsets - 1)
    def _():
        o_ref[0] = (acc_scr[...] / l_scr[...]).astype(o_ref.dtype)


def flash(need, qp, kt, kp, q_tiles, k_tiles, v_tiles, seg_rows, seg_cols, score_scale):
    slots, rows, width = q_tiles.shape
    offsets = 2 * REACH + 1
    kern = functools.partial(flash_kernel, offsets=offsets, score_scale=score_scale)
    grid_spec = pltpu.PrefetchScalarGridSpec(
        num_scalar_prefetch=4,
        grid=(slots, offsets),
        in_specs=[
            pl.BlockSpec((1, rows, width), lambda j, o, nd, qp, kt, kp: (j, 0, 0)),
            pl.BlockSpec((1, rows, width), lambda j, o, nd, qp, kt, kp: (kt[j * offsets + o], 0, 0)),
            pl.BlockSpec((1, rows, width), lambda j, o, nd, qp, kt, kp: (kt[j * offsets + o], 0, 0)),
            pl.BlockSpec((1, rows, 1), lambda j, o, nd, qp, kt, kp: (qp[j], 0, 0)),
            pl.BlockSpec((1, 1, rows), lambda j, o, nd, qp, kt, kp: (kp[j * offsets + o], 0, 0)),
        ],
        out_specs=pl.BlockSpec((1, rows, width), lambda j, o, nd, qp, kt, kp: (j, 0, 0)),
        scratch_shapes=[
            pltpu.VMEM((rows, 1), jnp.float32),
            pltpu.VMEM((rows, 1), jnp.float32),
            pltpu.VMEM((rows, width), jnp.float32),
        ],
    )
    return pl.pallas_call(
        kern,
        grid_spec=grid_spec,
        out_shape=jax.ShapeDtypeStruct((slots, rows, width), jnp.bfloat16),
        compiler_params=pltpu.CompilerParams(
            dimension_semantics=("arbitrary", "arbitrary")
        ),
    )(need, qp, kt, kp, q_tiles, k_tiles, v_tiles, seg_rows, seg_cols)


def doubling_gather(piece, me, size):
    held = piece[None]
    shift = 1
    while shift < size:
        came = lax.ppermute(held, "ctx", [(e, (e + shift) % size) for e in range(size)])
        held = jnp.concatenate([came, held], axis=0)
        shift *= 2
    return jnp.roll(held, me + 1, axis=0)


def relay_kernel(src_ref, dst_ref, send_sem, recv_sem, *, slots, size, inverse):
    me = lax.axis_index("ctx")
    barrier = pltpu.get_barrier_semaphore()
    for step in range(1, size):
        pl.semaphore_signal(
            barrier, inc=1, device_id={"ctx": lax.rem(me + step, size)},
            device_id_type=pl.DeviceIdType.MESH,
        )
    pl.semaphore_wait(barrier, size - 1)
    copies = []
    for j in range(slots):
        target = lax.rem(inverse * (me - j + size), size)
        head = (slots * target + j) // size
        remote = pltpu.make_async_remote_copy(
            src_ref.at[head], dst_ref.at[j], send_sem.at[j], recv_sem.at[j],
            device_id={"ctx": target}, device_id_type=pl.DeviceIdType.MESH,
        )
        here = pltpu.make_async_copy(src_ref.at[head], dst_ref.at[j], recv_sem.at[j])
        is_self = target == me

        @pl.when(is_self)
        def _():
            here.start()

        @pl.when(jnp.logical_not(is_self))
        def _():
            remote.start()

        copies.append((remote, here, is_self))
    for remote, here, is_self in copies:
        @pl.when(is_self)
        def _():
            here.wait()

        @pl.when(jnp.logical_not(is_self))
        def _():
            remote.wait_send()
            remote.wait_recv()


def relay(tiles, slots, size):
    inverse = pow(slots, -1, size)
    kern = functools.partial(relay_kernel, slots=slots, size=size, inverse=inverse)
    return pl.pallas_call(
        kern,
        out_shape=jax.ShapeDtypeStruct((slots,) + tiles.shape[1:], tiles.dtype),
        in_specs=[pl.BlockSpec(memory_space=pl.ANY)],
        out_specs=pl.BlockSpec(memory_space=pl.ANY),
        scratch_shapes=[pltpu.SemaphoreType.DMA((slots,)), pltpu.SemaphoreType.DMA((slots,))],
        compiler_params=pltpu.CompilerParams(collective_id=0, has_side_effects=True),
    )(tiles)


def local(
    query_raw,
    key_raw,
    value_rows,
    query_gain,
    key_gain,
    segment,
    destination,
    timestep,
    out_weight,
    gate_table,
):
    row_count = query_raw.shape[0]
    row_width = query_raw.shape[1]
    head_count = row_width // HD
    ctx_size = lax.axis_size("ctx")
    total_width = row_width * lax.axis_size("head")
    score_scale = 1.0 / math.sqrt(HD)
    me = lax.axis_index("ctx")
    tiles = head_count * ctx_size
    slots = tiles // ctx_size

    marks = doubling_gather(jnp.stack([segment, destination]), me, ctx_size)
    seg_blocks = marks[:, 0]
    dest_blocks = marks[:, 1]
    query_float = query_raw.astype(jnp.float32)
    key_float = key_raw.astype(jnp.float32)
    query_sum, key_sum = lax.psum(
        (jnp.sum(query_float * query_float, axis=1), jnp.sum(key_float * key_float, axis=1)), "head"
    )
    queries = (
        query_float * lax.rsqrt(query_sum / total_width + 1e-06)[:, None] * query_gain
    ).astype(jnp.bfloat16)
    normed_keys = (key_float * lax.rsqrt(key_sum / total_width + 1e-06)[:, None] * key_gain).astype(
        jnp.bfloat16
    )

    qkv = jnp.stack([queries, normed_keys, value_rows]).reshape(3, row_count, head_count, HD)
    qkv = jnp.transpose(qkv, (0, 2, 1, 3))

    came = relay(jnp.transpose(qkv, (1, 0, 2, 3)), slots, ctx_size)
    own = jnp.transpose(came, (1, 0, 2, 3))

    kv_own = own[1:]
    left = lax.ppermute(
        kv_own[:, slots - REACH:], "ctx", [(e, e + 1) for e in range(ctx_size - 1)]
    )
    right = lax.ppermute(
        kv_own[:, :REACH], "ctx", [(e, e - 1) for e in range(1, ctx_size)]
    )
    kv_all = jnp.concatenate([left, kv_own, right], axis=1)

    seg_lo = seg_blocks[:, 0]
    seg_hi = seg_blocks[:, -1]

    offsets = 2 * REACH + 1
    jj = jnp.arange(slots, dtype=jnp.int32)[:, None]
    oo = jnp.arange(offsets, dtype=jnp.int32)[None, :] - REACH
    t_q = slots * me + jj
    t_k = t_q + oo
    p_q = t_q % ctx_size
    valid = (t_k >= 0) & (t_k < tiles)
    t_kc = jnp.clip(t_k, 0, tiles - 1)
    p_k = t_kc % ctx_size
    same_head = (t_kc // ctx_size) == (t_q // ctx_size)
    meet = (seg_lo[p_q] <= seg_hi[p_k]) & (seg_lo[p_k] <= seg_hi[p_q])
    need_b = (valid & same_head & meet).reshape(-1)
    need = need_b.astype(jnp.int32)
    steps = jnp.arange(need.shape[0], dtype=jnp.int32)
    latest = lax.cummax(jnp.where(need_b, steps, -1), axis=0)
    source = jnp.where(latest < 0, jnp.argmax(need_b).astype(jnp.int32), latest)
    kt = (jj + oo + REACH).astype(jnp.int32).reshape(-1)[source]
    qp = p_q[:, 0].astype(jnp.int32)
    kp = p_k.astype(jnp.int32).reshape(-1)[source]

    attended = flash(
        need, qp, kt, kp,
        own[0], kv_all[0], kv_all[1],
        seg_blocks.reshape(ctx_size, row_count, 1),
        seg_blocks.reshape(ctx_size, 1, row_count),
        score_scale,
    )

    slot_count = row_count // ctx_size
    dest_mine = dest_blocks[qp]
    place = (dest_mine // row_count) * slot_count + dest_mine % slot_count
    chooser = (
        place[:, None, :] == jnp.arange(row_count, dtype=jnp.int32)[None, :, None]
    ).astype(jnp.bfloat16)
    placed = jnp.einsum(
        "jsr,jrd->jsd", chooser, attended, preferred_element_type=jnp.float32
    ).astype(jnp.bfloat16)
    placed = placed.reshape(slots, ctx_size, slot_count, HD).transpose(1, 0, 2, 3)
    got = lax.all_to_all(placed, "ctx", split_axis=0, concat_axis=0, tiled=True)
    got = got.reshape(head_count, ctx_size, slot_count, HD).transpose(1, 2, 0, 3)
    owned_attended = got.reshape(row_count, row_width)

    wanted = (
        me * row_count
        + jnp.arange(ctx_size, dtype=jnp.int32)[:, None, None] * slot_count
        + jnp.arange(slot_count, dtype=jnp.int32)[None, :, None]
    )
    owned_video = jnp.sum(
        jnp.where(dest_blocks[:, None, :] == wanted, seg_blocks[:, None, :], 0), axis=2
    ).reshape(row_count)

    head_terms = jnp.dot(owned_attended, out_weight, preferred_element_type=jnp.float32)
    mixed_rows = lax.psum_scatter(
        head_terms.astype(jnp.bfloat16), "head", scatter_dimension=1, tiled=True
    ).astype(jnp.float32)
    video_gates = jnp.dot(
        jax.nn.one_hot(timestep, gate_table.shape[0], dtype=jnp.float32),
        gate_table,
        precision=lax.Precision.HIGHEST,
    )
    token_gates = jnp.dot(
        jax.nn.one_hot(owned_video, timestep.shape[0], dtype=jnp.float32),
        video_gates,
        precision=lax.Precision.HIGHEST,
    )
    return (mixed_rows * token_gates).astype(jnp.bfloat16)


def solution(mesh):
    placed = (
        P(("batch", "ctx"), "head"),
        P(("batch", "ctx"), "head"),
        P(("batch", "ctx"), "head"),
        P("head"),
        P("head"),
        P(("batch", "ctx")),
        P(("batch", "ctx")),
        P("batch"),
        P("head", None),
        P(None, "head"),
    )
    return jax.shard_map(
        local, mesh=mesh, in_specs=placed, out_specs=P(("batch", "ctx"), "head"), check_vma=False
    )
```

```python
import functools
import math

import jax
import jax.numpy as jnp
from jax import lax
from jax.experimental import pallas as pl
from jax.experimental.pallas import tpu as pltpu
from jax.sharding import PartitionSpec as P

HD = 128
REACH = 4


def flash_kernel(
    need_ref, qp_ref, kt_ref, kp_ref,
    q_ref, k_ref, v_ref, qs_ref, ks_ref,
    o_ref, m_scr, l_scr, acc_scr, *, offsets, score_scale
):
    j = pl.program_id(0)
    o = pl.program_id(1)

    @pl.when(o == 0)
    def _():
        m_scr[...] = jnp.full_like(m_scr, -1e30)
        l_scr[...] = jnp.zeros_like(l_scr)
        acc_scr[...] = jnp.zeros_like(acc_scr)

    @pl.when(need_ref[j * offsets + o] != 0)
    def _():
        q = q_ref[0]
        k = k_ref[0]
        s = lax.dot_general(
            q, k, (((1,), (1,)), ((), ())), preferred_element_type=jnp.float32
        ) * score_scale
        mask = qs_ref[0] == ks_ref[0]
        s = jnp.where(mask, s, -1e30)
        m_prev = m_scr[...]
        m_new = jnp.maximum(m_prev, jnp.max(s, axis=1, keepdims=True))
        alpha = jnp.exp(m_prev - m_new)
        p = jnp.where(mask, jnp.exp(s - m_new), 0.0)
        l_scr[...] = alpha * l_scr[...] + jnp.sum(p, axis=1, keepdims=True)
        acc_scr[...] = alpha * acc_scr[...] + jnp.dot(
            p.astype(jnp.bfloat16), v_ref[0], preferred_element_type=jnp.float32
        )
        m_scr[...] = m_new

    @pl.when(o == offsets - 1)
    def _():
        o_ref[0] = (acc_scr[...] / l_scr[...]).astype(o_ref.dtype)


def flash(need, qp, kt, kp, q_tiles, k_tiles, v_tiles, seg_rows, seg_cols, score_scale):
    slots, rows, width = q_tiles.shape
    offsets = 2 * REACH + 1
    kern = functools.partial(flash_kernel, offsets=offsets, score_scale=score_scale)
    grid_spec = pltpu.PrefetchScalarGridSpec(
        num_scalar_prefetch=4,
        grid=(slots, offsets),
        in_specs=[
            pl.BlockSpec((1, rows, width), lambda j, o, nd, qp, kt, kp: (j, 0, 0)),
            pl.BlockSpec((1, rows, width), lambda j, o, nd, qp, kt, kp: (kt[j * offsets + o], 0, 0)),
            pl.BlockSpec((1, rows, width), lambda j, o, nd, qp, kt, kp: (kt[j * offsets + o], 0, 0)),
            pl.BlockSpec((1, rows, 1), lambda j, o, nd, qp, kt, kp: (qp[j], 0, 0)),
            pl.BlockSpec((1, 1, rows), lambda j, o, nd, qp, kt, kp: (kp[j * offsets + o], 0, 0)),
        ],
        out_specs=pl.BlockSpec((1, rows, width), lambda j, o, nd, qp, kt, kp: (j, 0, 0)),
        scratch_shapes=[
            pltpu.VMEM((rows, 1), jnp.float32),
            pltpu.VMEM((rows, 1), jnp.float32),
            pltpu.VMEM((rows, width), jnp.float32),
        ],
    )
    return pl.pallas_call(
        kern,
        grid_spec=grid_spec,
        out_shape=jax.ShapeDtypeStruct((slots, rows, width), jnp.bfloat16),
        compiler_params=pltpu.CompilerParams(
            dimension_semantics=("arbitrary", "arbitrary")
        ),
    )(need, qp, kt, kp, q_tiles, k_tiles, v_tiles, seg_rows, seg_cols)


def relay_kernel(src_ref, dst_ref, send_sem, recv_sem, *, slots, size, inverse):
    me = lax.axis_index("ctx")
    barrier = pltpu.get_barrier_semaphore()
    for step in range(1, size):
        pl.semaphore_signal(
            barrier, inc=1, device_id={"ctx": lax.rem(me + step, size)},
            device_id_type=pl.DeviceIdType.MESH,
        )
    pl.semaphore_wait(barrier, size - 1)
    copies = []
    for j in range(slots):
        target = lax.rem(inverse * (me - j + size), size)
        head = (slots * target + j) // size
        remote = pltpu.make_async_remote_copy(
            src_ref.at[head], dst_ref.at[j], send_sem.at[j], recv_sem.at[j],
            device_id={"ctx": target}, device_id_type=pl.DeviceIdType.MESH,
        )
        here = pltpu.make_async_copy(src_ref.at[head], dst_ref.at[j], recv_sem.at[j])
        is_self = target == me

        @pl.when(is_self)
        def _():
            here.start()

        @pl.when(jnp.logical_not(is_self))
        def _():
            remote.start()

        copies.append((remote, here, is_self))
    for remote, here, is_self in copies:
        @pl.when(is_self)
        def _():
            here.wait()

        @pl.when(jnp.logical_not(is_self))
        def _():
            remote.wait_send()
            remote.wait_recv()


def relay(tiles, slots, size):
    inverse = pow(slots, -1, size)
    kern = functools.partial(relay_kernel, slots=slots, size=size, inverse=inverse)
    return pl.pallas_call(
        kern,
        out_shape=jax.ShapeDtypeStruct((slots,) + tiles.shape[1:], tiles.dtype),
        in_specs=[pl.BlockSpec(memory_space=pl.ANY)],
        out_specs=pl.BlockSpec(memory_space=pl.ANY),
        scratch_shapes=[pltpu.SemaphoreType.DMA((slots,)), pltpu.SemaphoreType.DMA((slots,))],
        compiler_params=pltpu.CompilerParams(collective_id=0, has_side_effects=True),
    )(tiles)


def local(
    query_raw,
    key_raw,
    value_rows,
    query_gain,
    key_gain,
    segment,
    destination,
    timestep,
    out_weight,
    gate_table,
):
    row_count = query_raw.shape[0]
    row_width = query_raw.shape[1]
    head_count = row_width // HD
    ctx_size = lax.axis_size("ctx")
    total_width = row_width * lax.axis_size("head")
    score_scale = 1.0 / math.sqrt(HD)
    me = lax.axis_index("ctx")
    tiles = head_count * ctx_size
    slots = tiles // ctx_size

    query_float = query_raw.astype(jnp.float32)
    key_float = key_raw.astype(jnp.float32)
    query_sum, key_sum = lax.psum(
        (jnp.sum(query_float * query_float, axis=1), jnp.sum(key_float * key_float, axis=1)), "head"
    )
    queries = (
        query_float * lax.rsqrt(query_sum / total_width + 1e-06)[:, None] * query_gain
    ).astype(jnp.bfloat16)
    normed_keys = (key_float * lax.rsqrt(key_sum / total_width + 1e-06)[:, None] * key_gain).astype(
        jnp.bfloat16
    )

    qkv = jnp.stack([queries, normed_keys, value_rows]).reshape(3, row_count, head_count, HD)
    qkv = jnp.transpose(qkv, (0, 2, 1, 3))
    meta = jnp.stack([segment, destination // 64, destination % 64]).astype(jnp.bfloat16)
    meta = meta.reshape(-1, HD)
    body_rows = 3 * row_count
    pad = (-(body_rows + meta.shape[0])) % 16

    meta_rows = meta.shape[0]
    sendable = jnp.concatenate(
        [
            jnp.transpose(qkv, (1, 0, 2, 3)).reshape(head_count, body_rows, HD),
            jnp.broadcast_to(meta[None], (head_count, meta_rows, HD)),
            jnp.zeros((head_count, pad, HD), jnp.bfloat16),
        ],
        axis=1,
    )
    came = relay(sendable, slots, ctx_size)
    own = came[:, :body_rows].reshape(slots, 3, row_count, HD).transpose(1, 0, 2, 3)
    own_meta = came[:, body_rows:body_rows + meta_rows].reshape(slots, 3, row_count)
    own_meta = own_meta.transpose(1, 0, 2).astype(jnp.int32)
    seg_own = own_meta[0]
    dest_own = own_meta[1] * 64 + own_meta[2]

    kv_own = own[1:]
    seg_own_b = seg_own.astype(jnp.bfloat16).reshape(slots, row_count // HD, HD)
    halo_rows = 2 * REACH * row_count

    def halo(kv_part, seg_part):
        return jnp.concatenate(
            [kv_part.reshape(halo_rows, HD), seg_part.reshape(REACH * row_count // HD, HD)], axis=0
        )

    left = lax.ppermute(
        halo(kv_own[:, slots - REACH:], seg_own_b[slots - REACH:]),
        "ctx",
        [(e, e + 1) for e in range(ctx_size - 1)],
    )
    right = lax.ppermute(
        halo(kv_own[:, :REACH], seg_own_b[:REACH]),
        "ctx",
        [(e, e - 1) for e in range(1, ctx_size)],
    )

    def unpack(got):
        kv_part = got[:halo_rows].reshape(2, REACH, row_count, HD)
        seg_part = got[halo_rows:].reshape(REACH, row_count).astype(jnp.int32)
        return kv_part, seg_part

    left_kv, left_seg = unpack(left)
    right_kv, right_seg = unpack(right)
    kv_all = jnp.concatenate([left_kv, kv_own, right_kv], axis=1)
    seg_keys = jnp.concatenate([left_seg, seg_own, right_seg], axis=0)
    seg_lo = seg_keys[:, 0]
    seg_hi = seg_keys[:, -1]

    offsets = 2 * REACH + 1
    jj = jnp.arange(slots, dtype=jnp.int32)[:, None]
    oo = jnp.arange(offsets, dtype=jnp.int32)[None, :] - REACH
    t_q = slots * me + jj
    t_k = t_q + oo
    valid = (t_k >= 0) & (t_k < tiles)
    t_kc = jnp.clip(t_k, 0, tiles - 1)
    same_head = (t_kc // ctx_size) == (t_q // ctx_size)
    q_index = jj + REACH
    k_index = jj + oo + REACH
    meet = (seg_lo[q_index] <= seg_hi[k_index]) & (seg_lo[k_index] <= seg_hi[q_index])
    need_b = (valid & same_head & meet).reshape(-1)
    need = need_b.astype(jnp.int32)
    steps = jnp.arange(need.shape[0], dtype=jnp.int32)
    latest = lax.cummax(jnp.where(need_b, steps, -1), axis=0)
    source = jnp.where(latest < 0, jnp.argmax(need_b).astype(jnp.int32), latest)
    kt = k_index.astype(jnp.int32).reshape(-1)[source]
    qp = q_index[:, 0].astype(jnp.int32)
    kp = kt

    attended = flash(
        need, qp, kt, kp,
        own[0], kv_all[0], kv_all[1],
        seg_keys.reshape(-1, row_count, 1),
        seg_keys.reshape(-1, 1, row_count),
        score_scale,
    )

    slot_count = row_count // ctx_size
    place = (dest_own // row_count) * slot_count + dest_own % slot_count
    chooser = (
        place[:, None, :] == jnp.arange(row_count, dtype=jnp.int32)[None, :, None]
    ).astype(jnp.bfloat16)
    placed = jnp.einsum(
        "jsr,jrd->jsd", chooser, attended, preferred_element_type=jnp.float32
    ).astype(jnp.bfloat16)
    placed_seg = jnp.einsum(
        "jsr,jr->js", chooser, seg_own.astype(jnp.bfloat16), preferred_element_type=jnp.float32
    ).astype(jnp.bfloat16)
    placed = placed.reshape(slots, ctx_size, slot_count, HD).transpose(1, 0, 2, 3)
    placed = placed.reshape(ctx_size, slots * slot_count, HD)
    placed_seg = placed_seg.reshape(slots, ctx_size, slot_count).transpose(1, 0, 2)
    seg_width = slots * slot_count
    seg_rows_n = -(-seg_width // HD)
    placed_seg = jnp.pad(
        placed_seg.reshape(ctx_size, seg_width), ((0, 0), (0, seg_rows_n * HD - seg_width))
    ).reshape(ctx_size, seg_rows_n, HD)
    extra = (-(seg_width + seg_rows_n)) % 16
    payload = jnp.concatenate(
        [placed, placed_seg, jnp.zeros((ctx_size, extra, HD), jnp.bfloat16)], axis=1
    )
    got = lax.all_to_all(payload, "ctx", split_axis=0, concat_axis=0, tiled=True)
    got_att = got[:, :seg_width].reshape(tiles, slot_count, HD)
    got_att = got_att.reshape(head_count, ctx_size, slot_count, HD).transpose(1, 2, 0, 3)
    owned_attended = got_att.reshape(row_count, row_width)
    got_seg = got[:, seg_width:seg_width + seg_rows_n].reshape(ctx_size, seg_rows_n * HD)
    got_seg = got_seg[:, :seg_width].reshape(tiles, slot_count)
    owned_video = got_seg[:ctx_size].reshape(row_count).astype(jnp.int32)

    head_terms = jnp.dot(owned_attended, out_weight, preferred_element_type=jnp.float32)
    mixed_rows = lax.psum_scatter(
        head_terms.astype(jnp.bfloat16), "head", scatter_dimension=1, tiled=True
    ).astype(jnp.float32)
    video_gates = jnp.dot(
        jax.nn.one_hot(timestep, gate_table.shape[0], dtype=jnp.float32),
        gate_table,
        precision=lax.Precision.HIGHEST,
    )
    token_gates = jnp.dot(
        jax.nn.one_hot(owned_video, timestep.shape[0], dtype=jnp.float32),
        video_gates,
        precision=lax.Precision.HIGHEST,
    )
    return (mixed_rows * token_gates).astype(jnp.bfloat16)


def solution(mesh):
    placed = (
        P(("batch", "ctx"), "head"),
        P(("batch", "ctx"), "head"),
        P(("batch", "ctx"), "head"),
        P("head"),
        P("head"),
        P(("batch", "ctx")),
        P(("batch", "ctx")),
        P("batch"),
        P("head", None),
        P(None, "head"),
    )
    return jax.shard_map(
        local, mesh=mesh, in_specs=placed, out_specs=P(("batch", "ctx"), "head"), check_vma=False
    )
```

```python
import functools
import math

import jax
import jax.numpy as jnp
from jax import lax
from jax.experimental import pallas as pl
from jax.experimental.pallas import tpu as pltpu
from jax.sharding import PartitionSpec as P

HD = 128
REACH = 4


def flash_kernel(
    need_ref, qp_ref, kt_ref, kp_ref,
    q_ref, k_ref, v_ref, qs_ref, ks_ref,
    o_ref, m_scr, l_scr, acc_scr, *, offsets, score_scale
):
    j = pl.program_id(0)
    o = pl.program_id(1)

    @pl.when(o == 0)
    def _():
        m_scr[...] = jnp.full_like(m_scr, -1e30)
        l_scr[...] = jnp.zeros_like(l_scr)
        acc_scr[...] = jnp.zeros_like(acc_scr)

    @pl.when(need_ref[j * offsets + o] != 0)
    def _():
        q = q_ref[0]
        k = k_ref[0]
        s = lax.dot_general(
            q, k, (((1,), (1,)), ((), ())), preferred_element_type=jnp.float32
        ) * score_scale
        mask = qs_ref[0] == ks_ref[0]
        s = jnp.where(mask, s, -1e30)
        m_prev = m_scr[...]
        m_new = jnp.maximum(m_prev, jnp.max(s, axis=1, keepdims=True))
        alpha = jnp.exp(m_prev - m_new)
        p = jnp.where(mask, jnp.exp(s - m_new), 0.0)
        l_scr[...] = alpha * l_scr[...] + jnp.sum(p, axis=1, keepdims=True)
        acc_scr[...] = alpha * acc_scr[...] + jnp.dot(
            p.astype(jnp.bfloat16), v_ref[0], preferred_element_type=jnp.float32
        )
        m_scr[...] = m_new

    @pl.when(o == offsets - 1)
    def _():
        o_ref[0] = (acc_scr[...] / l_scr[...]).astype(o_ref.dtype)


def flash(need, qp, kt, kp, q_tiles, k_tiles, v_tiles, seg_rows, seg_cols, score_scale):
    slots, rows, width = q_tiles.shape
    offsets = 2 * REACH + 1
    kern = functools.partial(flash_kernel, offsets=offsets, score_scale=score_scale)
    grid_spec = pltpu.PrefetchScalarGridSpec(
        num_scalar_prefetch=4,
        grid=(slots, offsets),
        in_specs=[
            pl.BlockSpec((1, rows, width), lambda j, o, nd, qp, kt, kp: (j, 0, 0)),
            pl.BlockSpec((1, rows, width), lambda j, o, nd, qp, kt, kp: (kt[j * offsets + o], 0, 0)),
            pl.BlockSpec((1, rows, width), lambda j, o, nd, qp, kt, kp: (kt[j * offsets + o], 0, 0)),
            pl.BlockSpec((1, rows, 1), lambda j, o, nd, qp, kt, kp: (qp[j], 0, 0)),
            pl.BlockSpec((1, 1, rows), lambda j, o, nd, qp, kt, kp: (kp[j * offsets + o], 0, 0)),
        ],
        out_specs=pl.BlockSpec((1, rows, width), lambda j, o, nd, qp, kt, kp: (j, 0, 0)),
        scratch_shapes=[
            pltpu.VMEM((rows, 1), jnp.float32),
            pltpu.VMEM((rows, 1), jnp.float32),
            pltpu.VMEM((rows, width), jnp.float32),
        ],
    )
    return pl.pallas_call(
        kern,
        grid_spec=grid_spec,
        out_shape=jax.ShapeDtypeStruct((slots, rows, width), jnp.bfloat16),
        compiler_params=pltpu.CompilerParams(
            dimension_semantics=("arbitrary", "arbitrary")
        ),
    )(need, qp, kt, kp, q_tiles, k_tiles, v_tiles, seg_rows, seg_cols)


def relay_kernel(src_ref, mark_ref, dst_ref, marks_ref, send_sem, recv_sem, mark_send, mark_recv, self_sem,
                 *, slots, size, inverse):
    me = lax.axis_index("ctx")
    barrier = pltpu.get_barrier_semaphore()
    for step in range(1, size):
        pl.semaphore_signal(
            barrier, inc=1, device_id={"ctx": lax.rem(me + step, size)},
            device_id_type=pl.DeviceIdType.MESH,
        )
    pl.semaphore_wait(barrier, size - 1)
    copies = []
    for j in range(slots):
        target = lax.rem(inverse * (me - j + size), size)
        head = (slots * target + j) // size
        remote = pltpu.make_async_remote_copy(
            src_ref.at[head], dst_ref.at[j], send_sem.at[j], recv_sem.at[j],
            device_id={"ctx": target}, device_id_type=pl.DeviceIdType.MESH,
        )
        here = pltpu.make_async_copy(src_ref.at[head], dst_ref.at[j], recv_sem.at[j])
        is_self = target == me

        @pl.when(is_self)
        def _():
            here.start()

        @pl.when(jnp.logical_not(is_self))
        def _():
            remote.start()

        copies.append((remote, here, is_self))
    mark_copies = []
    for step in range(1, size):
        sent = pltpu.make_async_remote_copy(
            mark_ref, marks_ref.at[me], mark_send.at[step - 1], mark_recv.at[step - 1],
            device_id={"ctx": lax.rem(me + step, size)}, device_id_type=pl.DeviceIdType.MESH,
        )
        sent.start()
        mark_copies.append(sent)
    mine = pltpu.make_async_copy(mark_ref, marks_ref.at[me], self_sem.at[0])
    mine.start()
    for remote, here, is_self in copies:
        @pl.when(is_self)
        def _():
            here.wait()

        @pl.when(jnp.logical_not(is_self))
        def _():
            remote.wait_send()
            remote.wait_recv()

    for sent in mark_copies:
        sent.wait_send()
        sent.wait_recv()
    mine.wait()


def relay(tiles, marks, slots, size):
    inverse = pow(slots, -1, size)
    kern = functools.partial(relay_kernel, slots=slots, size=size, inverse=inverse)
    return pl.pallas_call(
        kern,
        out_shape=(
            jax.ShapeDtypeStruct((slots,) + tiles.shape[1:], tiles.dtype),
            jax.ShapeDtypeStruct((size,) + marks.shape, marks.dtype),
        ),
        in_specs=[pl.BlockSpec(memory_space=pl.ANY), pl.BlockSpec(memory_space=pl.ANY)],
        out_specs=(pl.BlockSpec(memory_space=pl.ANY), pl.BlockSpec(memory_space=pl.ANY)),
        scratch_shapes=[
            pltpu.SemaphoreType.DMA((slots,)),
            pltpu.SemaphoreType.DMA((slots,)),
            pltpu.SemaphoreType.DMA((size - 1,)),
            pltpu.SemaphoreType.DMA((size - 1,)),
            pltpu.SemaphoreType.DMA((1,)),
        ],
        compiler_params=pltpu.CompilerParams(collective_id=0, has_side_effects=True),
    )(tiles, marks)


def local(
    query_raw,
    key_raw,
    value_rows,
    query_gain,
    key_gain,
    segment,
    destination,
    timestep,
    out_weight,
    gate_table,
):
    row_count = query_raw.shape[0]
    row_width = query_raw.shape[1]
    head_count = row_width // HD
    ctx_size = lax.axis_size("ctx")
    total_width = row_width * lax.axis_size("head")
    score_scale = 1.0 / math.sqrt(HD)
    me = lax.axis_index("ctx")
    tiles = head_count * ctx_size
    slots = tiles // ctx_size

    query_float = query_raw.astype(jnp.float32)
    key_float = key_raw.astype(jnp.float32)
    query_sum, key_sum = lax.psum(
        (jnp.sum(query_float * query_float, axis=1), jnp.sum(key_float * key_float, axis=1)), "head"
    )
    queries = (
        query_float * lax.rsqrt(query_sum / total_width + 1e-06)[:, None] * query_gain
    ).astype(jnp.bfloat16)
    normed_keys = (key_float * lax.rsqrt(key_sum / total_width + 1e-06)[:, None] * key_gain).astype(
        jnp.bfloat16
    )

    qkv = jnp.stack([queries, normed_keys, value_rows]).reshape(3, row_count, head_count, HD)
    qkv = jnp.transpose(qkv, (0, 2, 1, 3))

    came, marks = relay(
        jnp.transpose(qkv, (1, 0, 2, 3)), jnp.stack([segment, destination]), slots, ctx_size
    )
    seg_blocks = marks[:, 0]
    dest_blocks = marks[:, 1]
    own = jnp.transpose(came, (1, 0, 2, 3))

    kv_own = own[1:]
    left = lax.ppermute(
        kv_own[:, slots - REACH:], "ctx", [(e, e + 1) for e in range(ctx_size - 1)]
    )
    right = lax.ppermute(
        kv_own[:, :REACH], "ctx", [(e, e - 1) for e in range(1, ctx_size)]
    )
    kv_all = jnp.concatenate([left, kv_own, right], axis=1)

    seg_lo = seg_blocks[:, 0]
    seg_hi = seg_blocks[:, -1]

    offsets = 2 * REACH + 1
    jj = jnp.arange(slots, dtype=jnp.int32)[:, None]
    oo = jnp.arange(offsets, dtype=jnp.int32)[None, :] - REACH
    t_q = slots * me + jj
    t_k = t_q + oo
    p_q = t_q % ctx_size
    valid = (t_k >= 0) & (t_k < tiles)
    t_kc = jnp.clip(t_k, 0, tiles - 1)
    p_k = t_kc % ctx_size
    same_head = (t_kc // ctx_size) == (t_q // ctx_size)
    meet = (seg_lo[p_q] <= seg_hi[p_k]) & (seg_lo[p_k] <= seg_hi[p_q])
    need_b = (valid & same_head & meet).reshape(-1)
    need = need_b.astype(jnp.int32)
    steps = jnp.arange(need.shape[0], dtype=jnp.int32)
    latest = lax.cummax(jnp.where(need_b, steps, -1), axis=0)
    source = jnp.where(latest < 0, jnp.argmax(need_b).astype(jnp.int32), latest)
    kt = (jj + oo + REACH).astype(jnp.int32).reshape(-1)[source]
    qp = p_q[:, 0].astype(jnp.int32)
    kp = p_k.astype(jnp.int32).reshape(-1)[source]

    attended = flash(
        need, qp, kt, kp,
        own[0], kv_all[0], kv_all[1],
        seg_blocks.reshape(ctx_size, row_count, 1),
        seg_blocks.reshape(ctx_size, 1, row_count),
        score_scale,
    )

    slot_count = row_count // ctx_size
    dest_mine = dest_blocks[qp]
    place = (dest_mine // row_count) * slot_count + dest_mine % slot_count
    chooser = (
        place[:, None, :] == jnp.arange(row_count, dtype=jnp.int32)[None, :, None]
    ).astype(jnp.bfloat16)
    placed = jnp.einsum(
        "jsr,jrd->jsd", chooser, attended, preferred_element_type=jnp.float32
    ).astype(jnp.bfloat16)
    placed = placed.reshape(slots, ctx_size, slot_count, HD).transpose(1, 0, 2, 3)
    got = lax.all_to_all(placed, "ctx", split_axis=0, concat_axis=0, tiled=True)
    got = got.reshape(head_count, ctx_size, slot_count, HD).transpose(1, 2, 0, 3)
    owned_attended = got.reshape(row_count, row_width)

    wanted = (
        me * row_count
        + jnp.arange(ctx_size, dtype=jnp.int32)[:, None, None] * slot_count
        + jnp.arange(slot_count, dtype=jnp.int32)[None, :, None]
    )
    owned_video = jnp.sum(
        jnp.where(dest_blocks[:, None, :] == wanted, seg_blocks[:, None, :], 0), axis=2
    ).reshape(row_count)

    head_terms = jnp.dot(owned_attended, out_weight, preferred_element_type=jnp.float32)
    mixed_rows = lax.psum_scatter(
        head_terms.astype(jnp.bfloat16), "head", scatter_dimension=1, tiled=True
    ).astype(jnp.float32)
    video_gates = jnp.dot(
        jax.nn.one_hot(timestep, gate_table.shape[0], dtype=jnp.float32),
        gate_table,
        precision=lax.Precision.HIGHEST,
    )
    token_gates = jnp.dot(
        jax.nn.one_hot(owned_video, timestep.shape[0], dtype=jnp.float32),
        video_gates,
        precision=lax.Precision.HIGHEST,
    )
    return (mixed_rows * token_gates).astype(jnp.bfloat16)


def solution(mesh):
    placed = (
        P(("batch", "ctx"), "head"),
        P(("batch", "ctx"), "head"),
        P(("batch", "ctx"), "head"),
        P("head"),
        P("head"),
        P(("batch", "ctx")),
        P(("batch", "ctx")),
        P("batch"),
        P("head", None),
        P(None, "head"),
    )
    return jax.shard_map(
        local, mesh=mesh, in_specs=placed, out_specs=P(("batch", "ctx"), "head"), check_vma=False
    )
```

```python
import functools
import math

import jax
import jax.numpy as jnp
from jax import lax
from jax.experimental import pallas as pl
from jax.experimental.pallas import tpu as pltpu
from jax.sharding import PartitionSpec as P

HD = 128
REACH = 4


def flash_kernel(
    need_ref, qp_ref, kt_ref, kp_ref,
    q_ref, k_ref, v_ref, qs_ref, ks_ref,
    o_ref, m_scr, l_scr, acc_scr, *, offsets, score_scale
):
    j = pl.program_id(0)
    o = pl.program_id(1)

    @pl.when(o == 0)
    def _():
        m_scr[...] = jnp.full_like(m_scr, -1e30)
        l_scr[...] = jnp.zeros_like(l_scr)
        acc_scr[...] = jnp.zeros_like(acc_scr)

    @pl.when(need_ref[j * offsets + o] != 0)
    def _():
        q = q_ref[0]
        k = k_ref[0]
        s = lax.dot_general(
            q, k, (((1,), (1,)), ((), ())), preferred_element_type=jnp.float32
        ) * score_scale
        mask = qs_ref[0] == ks_ref[0]
        s = jnp.where(mask, s, -1e30)
        m_prev = m_scr[...]
        m_new = jnp.maximum(m_prev, jnp.max(s, axis=1, keepdims=True))
        alpha = jnp.exp(m_prev - m_new)
        p = jnp.where(mask, jnp.exp(s - m_new), 0.0)
        l_scr[...] = alpha * l_scr[...] + jnp.sum(p, axis=1, keepdims=True)
        acc_scr[...] = alpha * acc_scr[...] + jnp.dot(
            p.astype(jnp.bfloat16), v_ref[0], preferred_element_type=jnp.float32
        )
        m_scr[...] = m_new

    @pl.when(o == offsets - 1)
    def _():
        o_ref[0] = (acc_scr[...] / l_scr[...]).astype(o_ref.dtype)


def flash(need, qp, kt, kp, q_tiles, k_tiles, v_tiles, seg_rows, seg_cols, score_scale):
    slots, rows, width = q_tiles.shape
    offsets = 2 * REACH + 1
    kern = functools.partial(flash_kernel, offsets=offsets, score_scale=score_scale)
    grid_spec = pltpu.PrefetchScalarGridSpec(
        num_scalar_prefetch=4,
        grid=(slots, offsets),
        in_specs=[
            pl.BlockSpec((1, rows, width), lambda j, o, nd, qp, kt, kp: (j, 0, 0)),
            pl.BlockSpec((1, rows, width), lambda j, o, nd, qp, kt, kp: (kt[j * offsets + o], 0, 0)),
            pl.BlockSpec((1, rows, width), lambda j, o, nd, qp, kt, kp: (kt[j * offsets + o], 0, 0)),
            pl.BlockSpec((1, rows, 1), lambda j, o, nd, qp, kt, kp: (qp[j], 0, 0)),
            pl.BlockSpec((1, 1, rows), lambda j, o, nd, qp, kt, kp: (kp[j * offsets + o], 0, 0)),
        ],
        out_specs=pl.BlockSpec((1, rows, width), lambda j, o, nd, qp, kt, kp: (j, 0, 0)),
        scratch_shapes=[
            pltpu.VMEM((rows, 1), jnp.float32),
            pltpu.VMEM((rows, 1), jnp.float32),
            pltpu.VMEM((rows, width), jnp.float32),
        ],
    )
    return pl.pallas_call(
        kern,
        grid_spec=grid_spec,
        out_shape=jax.ShapeDtypeStruct((slots, rows, width), jnp.bfloat16),
        compiler_params=pltpu.CompilerParams(
            dimension_semantics=("arbitrary", "arbitrary")
        ),
    )(need, qp, kt, kp, q_tiles, k_tiles, v_tiles, seg_rows, seg_cols)


def relay_kernel(src_ref, mark_ref, dst_ref, marks_ref, left_ref, right_ref,
                 send_sem, recv_sem, mark_send, mark_recv, self_sem, halo_send, halo_recv,
                 *, slots, size, inverse, reach):
    me = lax.axis_index("ctx")
    barrier = pltpu.get_barrier_semaphore()
    for step in range(1, size):
        pl.semaphore_signal(
            barrier, inc=1, device_id={"ctx": lax.rem(me + step, size)},
            device_id_type=pl.DeviceIdType.MESH,
        )
    pl.semaphore_wait(barrier, size - 1)
    copies = []
    for j in range(slots):
        target = lax.rem(inverse * (me - j + size), size)
        head = (slots * target + j) // size
        remote = pltpu.make_async_remote_copy(
            src_ref.at[head], dst_ref.at[j], send_sem.at[j], recv_sem.at[j],
            device_id={"ctx": target}, device_id_type=pl.DeviceIdType.MESH,
        )
        here = pltpu.make_async_copy(src_ref.at[head], dst_ref.at[j], recv_sem.at[j])
        is_self = target == me

        @pl.when(is_self)
        def _():
            here.start()

        @pl.when(jnp.logical_not(is_self))
        def _():
            remote.start()

        copies.append((remote, here, is_self))
    mark_copies = []
    for step in range(1, size):
        sent = pltpu.make_async_remote_copy(
            mark_ref, marks_ref.at[me], mark_send.at[step - 1], mark_recv.at[step - 1],
            device_id={"ctx": lax.rem(me + step, size)}, device_id_type=pl.DeviceIdType.MESH,
        )
        sent.start()
        mark_copies.append(sent)
    mine = pltpu.make_async_copy(mark_ref, marks_ref.at[me], self_sem.at[0])
    mine.start()
    for remote, here, is_self in copies:
        @pl.when(is_self)
        def _():
            here.wait()

        @pl.when(jnp.logical_not(is_self))
        def _():
            remote.wait_send()
            remote.wait_recv()

    for sent in mark_copies:
        sent.wait_send()
        sent.wait_recv()
    mine.wait()

    ahead = []
    for i in range(reach):
        to_next = pltpu.make_async_remote_copy(
            dst_ref.at[slots - reach + i, pl.ds(1, 2)], left_ref.at[i], halo_send.at[i], halo_recv.at[i],
            device_id={"ctx": jnp.minimum(me + 1, size - 1)}, device_id_type=pl.DeviceIdType.MESH,
        )
        to_prev = pltpu.make_async_remote_copy(
            dst_ref.at[i, pl.ds(1, 2)], right_ref.at[i], halo_send.at[reach + i], halo_recv.at[reach + i],
            device_id={"ctx": jnp.maximum(me - 1, 0)}, device_id_type=pl.DeviceIdType.MESH,
        )

        @pl.when(me < size - 1)
        def _():
            to_next.start()

        @pl.when(me > 0)
        def _():
            to_prev.start()

        ahead.append((to_next, to_prev))
    for to_next, to_prev in ahead:
        @pl.when(me < size - 1)
        def _():
            to_next.wait_send()

        @pl.when(me > 0)
        def _():
            to_next.wait_recv()

        @pl.when(me > 0)
        def _():
            to_prev.wait_send()

        @pl.when(me < size - 1)
        def _():
            to_prev.wait_recv()


def relay(tiles, marks, slots, size):
    inverse = pow(slots, -1, size)
    kern = functools.partial(relay_kernel, slots=slots, size=size, inverse=inverse, reach=REACH)
    halo_shape = jax.ShapeDtypeStruct((REACH, 2) + tiles.shape[2:], tiles.dtype)
    return pl.pallas_call(
        kern,
        out_shape=(
            jax.ShapeDtypeStruct((slots,) + tiles.shape[1:], tiles.dtype),
            jax.ShapeDtypeStruct((size,) + marks.shape, marks.dtype),
            halo_shape,
            halo_shape,
        ),
        in_specs=[pl.BlockSpec(memory_space=pl.ANY), pl.BlockSpec(memory_space=pl.ANY)],
        out_specs=tuple(pl.BlockSpec(memory_space=pl.ANY) for _ in range(4)),
        scratch_shapes=[
            pltpu.SemaphoreType.DMA((slots,)),
            pltpu.SemaphoreType.DMA((slots,)),
            pltpu.SemaphoreType.DMA((size - 1,)),
            pltpu.SemaphoreType.DMA((size - 1,)),
            pltpu.SemaphoreType.DMA((1,)),
            pltpu.SemaphoreType.DMA((2 * REACH,)),
            pltpu.SemaphoreType.DMA((2 * REACH,)),
        ],
        compiler_params=pltpu.CompilerParams(collective_id=0, has_side_effects=True),
    )(tiles, marks)


def local(
    query_raw,
    key_raw,
    value_rows,
    query_gain,
    key_gain,
    segment,
    destination,
    timestep,
    out_weight,
    gate_table,
):
    row_count = query_raw.shape[0]
    row_width = query_raw.shape[1]
    head_count = row_width // HD
    ctx_size = lax.axis_size("ctx")
    total_width = row_width * lax.axis_size("head")
    score_scale = 1.0 / math.sqrt(HD)
    me = lax.axis_index("ctx")
    tiles = head_count * ctx_size
    slots = tiles // ctx_size

    query_float = query_raw.astype(jnp.float32)
    key_float = key_raw.astype(jnp.float32)
    query_sum, key_sum = lax.psum(
        (jnp.sum(query_float * query_float, axis=1), jnp.sum(key_float * key_float, axis=1)), "head"
    )
    queries = (
        query_float * lax.rsqrt(query_sum / total_width + 1e-06)[:, None] * query_gain
    ).astype(jnp.bfloat16)
    normed_keys = (key_float * lax.rsqrt(key_sum / total_width + 1e-06)[:, None] * key_gain).astype(
        jnp.bfloat16
    )

    qkv = jnp.stack([queries, normed_keys, value_rows]).reshape(3, row_count, head_count, HD)
    qkv = jnp.transpose(qkv, (0, 2, 1, 3))

    came, marks, left_got, right_got = relay(
        jnp.transpose(qkv, (1, 0, 2, 3)), jnp.stack([segment, destination]), slots, ctx_size
    )
    seg_blocks = marks[:, 0]
    dest_blocks = marks[:, 1]
    own = jnp.transpose(came, (1, 0, 2, 3))

    kv_own = own[1:]
    left = jnp.transpose(left_got, (1, 0, 2, 3))
    right = jnp.transpose(right_got, (1, 0, 2, 3))
    kv_all = jnp.concatenate([left, kv_own, right], axis=1)

    seg_lo = seg_blocks[:, 0]
    seg_hi = seg_blocks[:, -1]

    offsets = 2 * REACH + 1
    jj = jnp.arange(slots, dtype=jnp.int32)[:, None]
    oo = jnp.arange(offsets, dtype=jnp.int32)[None, :] - REACH
    t_q = slots * me + jj
    t_k = t_q + oo
    p_q = t_q % ctx_size
    valid = (t_k >= 0) & (t_k < tiles)
    t_kc = jnp.clip(t_k, 0, tiles - 1)
    p_k = t_kc % ctx_size
    same_head = (t_kc // ctx_size) == (t_q // ctx_size)
    meet = (seg_lo[p_q] <= seg_hi[p_k]) & (seg_lo[p_k] <= seg_hi[p_q])
    need_b = (valid & same_head & meet).reshape(-1)
    need = need_b.astype(jnp.int32)
    steps = jnp.arange(need.shape[0], dtype=jnp.int32)
    latest = lax.cummax(jnp.where(need_b, steps, -1), axis=0)
    source = jnp.where(latest < 0, jnp.argmax(need_b).astype(jnp.int32), latest)
    kt = (jj + oo + REACH).astype(jnp.int32).reshape(-1)[source]
    qp = p_q[:, 0].astype(jnp.int32)
    kp = p_k.astype(jnp.int32).reshape(-1)[source]

    attended = flash(
        need, qp, kt, kp,
        own[0], kv_all[0], kv_all[1],
        seg_blocks.reshape(ctx_size, row_count, 1),
        seg_blocks.reshape(ctx_size, 1, row_count),
        score_scale,
    )

    slot_count = row_count // ctx_size
    dest_mine = dest_blocks[qp]
    place = (dest_mine // row_count) * slot_count + dest_mine % slot_count
    chooser = (
        place[:, None, :] == jnp.arange(row_count, dtype=jnp.int32)[None, :, None]
    ).astype(jnp.bfloat16)
    placed = jnp.einsum(
        "jsr,jrd->jsd", chooser, attended, preferred_element_type=jnp.float32
    ).astype(jnp.bfloat16)
    placed = placed.reshape(slots, ctx_size, slot_count, HD).transpose(1, 0, 2, 3)
    got = lax.all_to_all(placed, "ctx", split_axis=0, concat_axis=0, tiled=True)
    got = got.reshape(head_count, ctx_size, slot_count, HD).transpose(1, 2, 0, 3)
    owned_attended = got.reshape(row_count, row_width)

    wanted = (
        me * row_count
        + jnp.arange(ctx_size, dtype=jnp.int32)[:, None, None] * slot_count
        + jnp.arange(slot_count, dtype=jnp.int32)[None, :, None]
    )
    owned_video = jnp.sum(
        jnp.where(dest_blocks[:, None, :] == wanted, seg_blocks[:, None, :], 0), axis=2
    ).reshape(row_count)

    head_terms = jnp.dot(owned_attended, out_weight, preferred_element_type=jnp.float32)
    mixed_rows = lax.psum_scatter(
        head_terms.astype(jnp.bfloat16), "head", scatter_dimension=1, tiled=True
    ).astype(jnp.float32)
    video_gates = jnp.dot(
        jax.nn.one_hot(timestep, gate_table.shape[0], dtype=jnp.float32),
        gate_table,
        precision=lax.Precision.HIGHEST,
    )
    token_gates = jnp.dot(
        jax.nn.one_hot(owned_video, timestep.shape[0], dtype=jnp.float32),
        video_gates,
        precision=lax.Precision.HIGHEST,
    )
    return (mixed_rows * token_gates).astype(jnp.bfloat16)


def solution(mesh):
    placed = (
        P(("batch", "ctx"), "head"),
        P(("batch", "ctx"), "head"),
        P(("batch", "ctx"), "head"),
        P("head"),
        P("head"),
        P(("batch", "ctx")),
        P(("batch", "ctx")),
        P("batch"),
        P("head", None),
        P(None, "head"),
    )
    return jax.shard_map(
        local, mesh=mesh, in_specs=placed, out_specs=P(("batch", "ctx"), "head"), check_vma=False
    )
```

```python
import functools
import math

import jax
import jax.numpy as jnp
from jax import lax
from jax.experimental import pallas as pl
from jax.experimental.pallas import tpu as pltpu
from jax.sharding import PartitionSpec as P

HD = 128
REACH = 4


def flash_kernel(
    need_ref, qp_ref, kt_ref, kp_ref,
    q_ref, k_ref, v_ref, qs_ref, ks_ref,
    o_ref, m_scr, l_scr, acc_scr, *, offsets, score_scale
):
    j = pl.program_id(0)
    o = pl.program_id(1)

    @pl.when(o == 0)
    def _():
        m_scr[...] = jnp.full_like(m_scr, -1e30)
        l_scr[...] = jnp.zeros_like(l_scr)
        acc_scr[...] = jnp.zeros_like(acc_scr)

    def step(masked):
        q = q_ref[0]
        k = k_ref[0]
        s = lax.dot_general(
            q, k, (((1,), (1,)), ((), ())), preferred_element_type=jnp.float32
        ) * score_scale
        if masked:
            mask = qs_ref[0] == ks_ref[0]
            s = jnp.where(mask, s, -1e30)
        m_prev = m_scr[...]
        m_new = jnp.maximum(m_prev, jnp.max(s, axis=1, keepdims=True))
        alpha = jnp.exp(m_prev - m_new)
        p = jnp.exp(s - m_new)
        if masked:
            p = jnp.where(mask, p, 0.0)
        l_scr[...] = alpha * l_scr[...] + jnp.sum(p, axis=1, keepdims=True)
        acc_scr[...] = alpha * acc_scr[...] + jnp.dot(
            p.astype(jnp.bfloat16), v_ref[0], preferred_element_type=jnp.float32
        )
        m_scr[...] = m_new

    @pl.when(need_ref[j * offsets + o] == 1)
    def _():
        step(True)

    @pl.when(need_ref[j * offsets + o] == 2)
    def _():
        step(False)

    @pl.when(o == offsets - 1)
    def _():
        o_ref[0] = (acc_scr[...] / l_scr[...]).astype(o_ref.dtype)


def flash(need, qp, kt, kp, q_tiles, k_tiles, v_tiles, seg_rows, seg_cols, score_scale):
    slots, rows, width = q_tiles.shape
    offsets = 2 * REACH + 1
    kern = functools.partial(flash_kernel, offsets=offsets, score_scale=score_scale)
    grid_spec = pltpu.PrefetchScalarGridSpec(
        num_scalar_prefetch=4,
        grid=(slots, offsets),
        in_specs=[
            pl.BlockSpec((1, rows, width), lambda j, o, nd, qp, kt, kp: (j, 0, 0)),
            pl.BlockSpec((1, rows, width), lambda j, o, nd, qp, kt, kp: (kt[j * offsets + o], 0, 0)),
            pl.BlockSpec((1, rows, width), lambda j, o, nd, qp, kt, kp: (kt[j * offsets + o], 0, 0)),
            pl.BlockSpec((1, rows, 1), lambda j, o, nd, qp, kt, kp: (qp[j], 0, 0)),
            pl.BlockSpec((1, 1, rows), lambda j, o, nd, qp, kt, kp: (kp[j * offsets + o], 0, 0)),
        ],
        out_specs=pl.BlockSpec((1, rows, width), lambda j, o, nd, qp, kt, kp: (j, 0, 0)),
        scratch_shapes=[
            pltpu.VMEM((rows, 1), jnp.float32),
            pltpu.VMEM((rows, 1), jnp.float32),
            pltpu.VMEM((rows, width), jnp.float32),
        ],
    )
    return pl.pallas_call(
        kern,
        grid_spec=grid_spec,
        out_shape=jax.ShapeDtypeStruct((slots, rows, width), jnp.bfloat16),
        compiler_params=pltpu.CompilerParams(
            dimension_semantics=("arbitrary", "arbitrary")
        ),
    )(need, qp, kt, kp, q_tiles, k_tiles, v_tiles, seg_rows, seg_cols)


def relay_kernel(src_ref, mark_ref, dst_ref, marks_ref, send_sem, recv_sem, mark_send, mark_recv, self_sem,
                 *, slots, size, inverse):
    me = lax.axis_index("ctx")
    barrier = pltpu.get_barrier_semaphore()
    for step in range(1, size):
        pl.semaphore_signal(
            barrier, inc=1, device_id={"ctx": lax.rem(me + step, size)},
            device_id_type=pl.DeviceIdType.MESH,
        )
    pl.semaphore_wait(barrier, size - 1)
    copies = []
    for j in range(slots):
        target = lax.rem(inverse * (me - j + size), size)
        head = (slots * target + j) // size
        remote = pltpu.make_async_remote_copy(
            src_ref.at[head], dst_ref.at[j], send_sem.at[j], recv_sem.at[j],
            device_id={"ctx": target}, device_id_type=pl.DeviceIdType.MESH,
        )
        here = pltpu.make_async_copy(src_ref.at[head], dst_ref.at[j], recv_sem.at[j])
        is_self = target == me

        @pl.when(is_self)
        def _():
            here.start()

        @pl.when(jnp.logical_not(is_self))
        def _():
            remote.start()

        copies.append((remote, here, is_self))
    mark_copies = []
    for step in range(1, size):
        sent = pltpu.make_async_remote_copy(
            mark_ref, marks_ref.at[me], mark_send.at[step - 1], mark_recv.at[step - 1],
            device_id={"ctx": lax.rem(me + step, size)}, device_id_type=pl.DeviceIdType.MESH,
        )
        sent.start()
        mark_copies.append(sent)
    mine = pltpu.make_async_copy(mark_ref, marks_ref.at[me], self_sem.at[0])
    mine.start()
    for remote, here, is_self in copies:
        @pl.when(is_self)
        def _():
            here.wait()

        @pl.when(jnp.logical_not(is_self))
        def _():
            remote.wait_send()
            remote.wait_recv()

    for sent in mark_copies:
        sent.wait_send()
        sent.wait_recv()
    mine.wait()


def relay(tiles, marks, slots, size):
    inverse = pow(slots, -1, size)
    kern = functools.partial(relay_kernel, slots=slots, size=size, inverse=inverse)
    return pl.pallas_call(
        kern,
        out_shape=(
            jax.ShapeDtypeStruct((slots,) + tiles.shape[1:], tiles.dtype),
            jax.ShapeDtypeStruct((size,) + marks.shape, marks.dtype),
        ),
        in_specs=[pl.BlockSpec(memory_space=pl.ANY), pl.BlockSpec(memory_space=pl.ANY)],
        out_specs=(pl.BlockSpec(memory_space=pl.ANY), pl.BlockSpec(memory_space=pl.ANY)),
        scratch_shapes=[
            pltpu.SemaphoreType.DMA((slots,)),
            pltpu.SemaphoreType.DMA((slots,)),
            pltpu.SemaphoreType.DMA((size - 1,)),
            pltpu.SemaphoreType.DMA((size - 1,)),
            pltpu.SemaphoreType.DMA((1,)),
        ],
        compiler_params=pltpu.CompilerParams(collective_id=0, has_side_effects=True),
    )(tiles, marks)


def local(
    query_raw,
    key_raw,
    value_rows,
    query_gain,
    key_gain,
    segment,
    destination,
    timestep,
    out_weight,
    gate_table,
):
    row_count = query_raw.shape[0]
    row_width = query_raw.shape[1]
    head_count = row_width // HD
    ctx_size = lax.axis_size("ctx")
    total_width = row_width * lax.axis_size("head")
    score_scale = 1.0 / math.sqrt(HD)
    me = lax.axis_index("ctx")
    tiles = head_count * ctx_size
    slots = tiles // ctx_size

    query_float = query_raw.astype(jnp.float32)
    key_float = key_raw.astype(jnp.float32)
    query_sum, key_sum = lax.psum(
        (jnp.sum(query_float * query_float, axis=1), jnp.sum(key_float * key_float, axis=1)), "head"
    )
    queries = (
        query_float * lax.rsqrt(query_sum / total_width + 1e-06)[:, None] * query_gain
    ).astype(jnp.bfloat16)
    normed_keys = (key_float * lax.rsqrt(key_sum / total_width + 1e-06)[:, None] * key_gain).astype(
        jnp.bfloat16
    )

    qkv = jnp.stack([queries, normed_keys, value_rows]).reshape(3, row_count, head_count, HD)
    qkv = jnp.transpose(qkv, (0, 2, 1, 3))

    came, marks = relay(
        jnp.transpose(qkv, (1, 0, 2, 3)), jnp.stack([segment, destination]), slots, ctx_size
    )
    seg_blocks = marks[:, 0]
    dest_blocks = marks[:, 1]
    own = jnp.transpose(came, (1, 0, 2, 3))

    kv_own = own[1:]
    left = lax.ppermute(
        kv_own[:, slots - REACH:], "ctx", [(e, e + 1) for e in range(ctx_size - 1)]
    )
    right = lax.ppermute(
        kv_own[:, :REACH], "ctx", [(e, e - 1) for e in range(1, ctx_size)]
    )
    kv_all = jnp.concatenate([left, kv_own, right], axis=1)

    seg_lo = seg_blocks[:, 0]
    seg_hi = seg_blocks[:, -1]

    offsets = 2 * REACH + 1
    jj = jnp.arange(slots, dtype=jnp.int32)[:, None]
    oo = jnp.arange(offsets, dtype=jnp.int32)[None, :] - REACH
    t_q = slots * me + jj
    t_k = t_q + oo
    p_q = t_q % ctx_size
    valid = (t_k >= 0) & (t_k < tiles)
    t_kc = jnp.clip(t_k, 0, tiles - 1)
    p_k = t_kc % ctx_size
    same_head = (t_kc // ctx_size) == (t_q // ctx_size)
    meet = (seg_lo[p_q] <= seg_hi[p_k]) & (seg_lo[p_k] <= seg_hi[p_q])
    need_b = (valid & same_head & meet).reshape(-1)
    whole = (
        (seg_lo[p_q] == seg_hi[p_q]) & (seg_lo[p_k] == seg_hi[p_k]) & (seg_lo[p_q] == seg_lo[p_k])
    ).reshape(-1)
    need = need_b.astype(jnp.int32) * (1 + whole.astype(jnp.int32))
    steps = jnp.arange(need.shape[0], dtype=jnp.int32)
    latest = lax.cummax(jnp.where(need_b, steps, -1), axis=0)
    source = jnp.where(latest < 0, jnp.argmax(need_b).astype(jnp.int32), latest)
    kt = (jj + oo + REACH).astype(jnp.int32).reshape(-1)[source]
    qp = p_q[:, 0].astype(jnp.int32)
    kp = p_k.astype(jnp.int32).reshape(-1)[source]

    attended = flash(
        need, qp, kt, kp,
        own[0], kv_all[0], kv_all[1],
        seg_blocks.reshape(ctx_size, row_count, 1),
        seg_blocks.reshape(ctx_size, 1, row_count),
        score_scale,
    )

    slot_count = row_count // ctx_size
    dest_mine = dest_blocks[qp]
    place = (dest_mine // row_count) * slot_count + dest_mine % slot_count
    chooser = (
        place[:, None, :] == jnp.arange(row_count, dtype=jnp.int32)[None, :, None]
    ).astype(jnp.bfloat16)
    placed = jnp.einsum(
        "jsr,jrd->jsd", chooser, attended, preferred_element_type=jnp.float32
    ).astype(jnp.bfloat16)
    placed = placed.reshape(slots, ctx_size, slot_count, HD).transpose(1, 0, 2, 3)
    got = lax.all_to_all(placed, "ctx", split_axis=0, concat_axis=0, tiled=True)
    got = got.reshape(head_count, ctx_size, slot_count, HD).transpose(1, 2, 0, 3)
    owned_attended = got.reshape(row_count, row_width)

    wanted = (
        me * row_count
        + jnp.arange(ctx_size, dtype=jnp.int32)[:, None, None] * slot_count
        + jnp.arange(slot_count, dtype=jnp.int32)[None, :, None]
    )
    owned_video = jnp.sum(
        jnp.where(dest_blocks[:, None, :] == wanted, seg_blocks[:, None, :], 0), axis=2
    ).reshape(row_count)

    head_terms = jnp.dot(owned_attended, out_weight, preferred_element_type=jnp.float32)
    mixed_rows = lax.psum_scatter(
        head_terms.astype(jnp.bfloat16), "head", scatter_dimension=1, tiled=True
    ).astype(jnp.float32)
    video_gates = jnp.dot(
        jax.nn.one_hot(timestep, gate_table.shape[0], dtype=jnp.float32),
        gate_table,
        precision=lax.Precision.HIGHEST,
    )
    token_gates = jnp.dot(
        jax.nn.one_hot(owned_video, timestep.shape[0], dtype=jnp.float32),
        video_gates,
        precision=lax.Precision.HIGHEST,
    )
    return (mixed_rows * token_gates).astype(jnp.bfloat16)


def solution(mesh):
    placed = (
        P(("batch", "ctx"), "head"),
        P(("batch", "ctx"), "head"),
        P(("batch", "ctx"), "head"),
        P("head"),
        P("head"),
        P(("batch", "ctx")),
        P(("batch", "ctx")),
        P("batch"),
        P("head", None),
        P(None, "head"),
    )
    return jax.shard_map(
        local, mesh=mesh, in_specs=placed, out_specs=P(("batch", "ctx"), "head"), check_vma=False
    )
```

```python
import functools
import math

import jax
import jax.numpy as jnp
from jax import lax
from jax.experimental import pallas as pl
from jax.experimental.pallas import tpu as pltpu
from jax.sharding import PartitionSpec as P

HD = 128
REACH = 4


def flash_kernel(
    need_ref, qp_ref, kt_ref, kp_ref,
    q_ref, k_ref, v_ref, qs_ref, ks_ref,
    o_ref, m_scr, l_scr, acc_scr, *, offsets, score_scale
):
    j = pl.program_id(0)
    o = pl.program_id(1)

    @pl.when(o == 0)
    def _():
        m_scr[...] = jnp.full_like(m_scr, -1e30)
        l_scr[...] = jnp.zeros_like(l_scr)
        acc_scr[...] = jnp.zeros_like(acc_scr)

    def step(masked):
        q = q_ref[0]
        k = k_ref[0]
        s = lax.dot_general(
            q, k, (((1,), (1,)), ((), ())), preferred_element_type=jnp.float32
        ) * score_scale
        if masked:
            mask = qs_ref[0] == ks_ref[0]
            s = jnp.where(mask, s, -1e30)
        m_prev = m_scr[...]
        m_new = jnp.maximum(m_prev, jnp.max(s, axis=1, keepdims=True))
        alpha = jnp.exp(m_prev - m_new)
        p = jnp.exp(s - m_new[:, :1])
        if masked:
            p = jnp.where(mask, p, 0.0)
        l_scr[...] = alpha * l_scr[...] + jnp.sum(p, axis=1, keepdims=True)
        acc_scr[...] = alpha * acc_scr[...] + jnp.dot(
            p.astype(jnp.bfloat16), v_ref[0], preferred_element_type=jnp.float32
        )
        m_scr[...] = m_new

    @pl.when(need_ref[j * offsets + o] == 1)
    def _():
        step(True)

    @pl.when(need_ref[j * offsets + o] == 2)
    def _():
        step(False)

    @pl.when(o == offsets - 1)
    def _():
        o_ref[0] = (acc_scr[...] / l_scr[...]).astype(o_ref.dtype)


def flash(need, qp, kt, kp, q_tiles, k_tiles, v_tiles, seg_rows, seg_cols, score_scale):
    slots, rows, width = q_tiles.shape
    offsets = 2 * REACH + 1
    kern = functools.partial(flash_kernel, offsets=offsets, score_scale=score_scale)
    grid_spec = pltpu.PrefetchScalarGridSpec(
        num_scalar_prefetch=4,
        grid=(slots, offsets),
        in_specs=[
            pl.BlockSpec((1, rows, width), lambda j, o, nd, qp, kt, kp: (j, 0, 0)),
            pl.BlockSpec((1, rows, width), lambda j, o, nd, qp, kt, kp: (kt[j * offsets + o], 0, 0)),
            pl.BlockSpec((1, rows, width), lambda j, o, nd, qp, kt, kp: (kt[j * offsets + o], 0, 0)),
            pl.BlockSpec((1, rows, 1), lambda j, o, nd, qp, kt, kp: (qp[j], 0, 0)),
            pl.BlockSpec((1, 1, rows), lambda j, o, nd, qp, kt, kp: (kp[j * offsets + o], 0, 0)),
        ],
        out_specs=pl.BlockSpec((1, rows, width), lambda j, o, nd, qp, kt, kp: (j, 0, 0)),
        scratch_shapes=[
            pltpu.VMEM((rows, width), jnp.float32),
            pltpu.VMEM((rows, width), jnp.float32),
            pltpu.VMEM((rows, width), jnp.float32),
        ],
    )
    return pl.pallas_call(
        kern,
        grid_spec=grid_spec,
        out_shape=jax.ShapeDtypeStruct((slots, rows, width), jnp.bfloat16),
        compiler_params=pltpu.CompilerParams(
            dimension_semantics=("arbitrary", "arbitrary")
        ),
    )(need, qp, kt, kp, q_tiles, k_tiles, v_tiles, seg_rows, seg_cols)


def relay_kernel(src_ref, mark_ref, dst_ref, marks_ref, send_sem, recv_sem, mark_send, mark_recv, self_sem,
                 *, slots, size, inverse):
    me = lax.axis_index("ctx")
    barrier = pltpu.get_barrier_semaphore()
    for step in range(1, size):
        pl.semaphore_signal(
            barrier, inc=1, device_id={"ctx": lax.rem(me + step, size)},
            device_id_type=pl.DeviceIdType.MESH,
        )
    pl.semaphore_wait(barrier, size - 1)
    copies = []
    for j in range(slots):
        target = lax.rem(inverse * (me - j + size), size)
        head = (slots * target + j) // size
        remote = pltpu.make_async_remote_copy(
            src_ref.at[head], dst_ref.at[j], send_sem.at[j], recv_sem.at[j],
            device_id={"ctx": target}, device_id_type=pl.DeviceIdType.MESH,
        )
        here = pltpu.make_async_copy(src_ref.at[head], dst_ref.at[j], recv_sem.at[j])
        is_self = target == me

        @pl.when(is_self)
        def _():
            here.start()

        @pl.when(jnp.logical_not(is_self))
        def _():
            remote.start()

        copies.append((remote, here, is_self))
    mark_copies = []
    for step in range(1, size):
        sent = pltpu.make_async_remote_copy(
            mark_ref, marks_ref.at[me], mark_send.at[step - 1], mark_recv.at[step - 1],
            device_id={"ctx": lax.rem(me + step, size)}, device_id_type=pl.DeviceIdType.MESH,
        )
        sent.start()
        mark_copies.append(sent)
    mine = pltpu.make_async_copy(mark_ref, marks_ref.at[me], self_sem.at[0])
    mine.start()
    for remote, here, is_self in copies:
        @pl.when(is_self)
        def _():
            here.wait()

        @pl.when(jnp.logical_not(is_self))
        def _():
            remote.wait_send()
            remote.wait_recv()

    for sent in mark_copies:
        sent.wait_send()
        sent.wait_recv()
    mine.wait()


def relay(tiles, marks, slots, size):
    inverse = pow(slots, -1, size)
    kern = functools.partial(relay_kernel, slots=slots, size=size, inverse=inverse)
    return pl.pallas_call(
        kern,
        out_shape=(
            jax.ShapeDtypeStruct((slots,) + tiles.shape[1:], tiles.dtype),
            jax.ShapeDtypeStruct((size,) + marks.shape, marks.dtype),
        ),
        in_specs=[pl.BlockSpec(memory_space=pl.ANY), pl.BlockSpec(memory_space=pl.ANY)],
        out_specs=(pl.BlockSpec(memory_space=pl.ANY), pl.BlockSpec(memory_space=pl.ANY)),
        scratch_shapes=[
            pltpu.SemaphoreType.DMA((slots,)),
            pltpu.SemaphoreType.DMA((slots,)),
            pltpu.SemaphoreType.DMA((size - 1,)),
            pltpu.SemaphoreType.DMA((size - 1,)),
            pltpu.SemaphoreType.DMA((1,)),
        ],
        compiler_params=pltpu.CompilerParams(collective_id=0, has_side_effects=True),
    )(tiles, marks)


def local(
    query_raw,
    key_raw,
    value_rows,
    query_gain,
    key_gain,
    segment,
    destination,
    timestep,
    out_weight,
    gate_table,
):
    row_count = query_raw.shape[0]
    row_width = query_raw.shape[1]
    head_count = row_width // HD
    ctx_size = lax.axis_size("ctx")
    total_width = row_width * lax.axis_size("head")
    score_scale = 1.0 / math.sqrt(HD)
    me = lax.axis_index("ctx")
    tiles = head_count * ctx_size
    slots = tiles // ctx_size

    query_float = query_raw.astype(jnp.float32)
    key_float = key_raw.astype(jnp.float32)
    query_sum, key_sum = lax.psum(
        (jnp.sum(query_float * query_float, axis=1), jnp.sum(key_float * key_float, axis=1)), "head"
    )
    queries = (
        query_float * lax.rsqrt(query_sum / total_width + 1e-06)[:, None] * query_gain
    ).astype(jnp.bfloat16)
    normed_keys = (key_float * lax.rsqrt(key_sum / total_width + 1e-06)[:, None] * key_gain).astype(
        jnp.bfloat16
    )

    qkv = jnp.stack([queries, normed_keys, value_rows]).reshape(3, row_count, head_count, HD)
    qkv = jnp.transpose(qkv, (0, 2, 1, 3))

    came, marks = relay(
        jnp.transpose(qkv, (1, 0, 2, 3)), jnp.stack([segment, destination]), slots, ctx_size
    )
    seg_blocks = marks[:, 0]
    dest_blocks = marks[:, 1]
    own = jnp.transpose(came, (1, 0, 2, 3))

    kv_own = own[1:]
    left = lax.ppermute(
        kv_own[:, slots - REACH:], "ctx", [(e, e + 1) for e in range(ctx_size - 1)]
    )
    right = lax.ppermute(
        kv_own[:, :REACH], "ctx", [(e, e - 1) for e in range(1, ctx_size)]
    )
    kv_all = jnp.concatenate([left, kv_own, right], axis=1)

    seg_lo = seg_blocks[:, 0]
    seg_hi = seg_blocks[:, -1]

    offsets = 2 * REACH + 1
    jj = jnp.arange(slots, dtype=jnp.int32)[:, None]
    oo = jnp.arange(offsets, dtype=jnp.int32)[None, :] - REACH
    t_q = slots * me + jj
    t_k = t_q + oo
    p_q = t_q % ctx_size
    valid = (t_k >= 0) & (t_k < tiles)
    t_kc = jnp.clip(t_k, 0, tiles - 1)
    p_k = t_kc % ctx_size
    same_head = (t_kc // ctx_size) == (t_q // ctx_size)
    meet = (seg_lo[p_q] <= seg_hi[p_k]) & (seg_lo[p_k] <= seg_hi[p_q])
    need_b = (valid & same_head & meet).reshape(-1)
    whole = (
        (seg_lo[p_q] == seg_hi[p_q]) & (seg_lo[p_k] == seg_hi[p_k]) & (seg_lo[p_q] == seg_lo[p_k])
    ).reshape(-1)
    need = need_b.astype(jnp.int32) * (1 + whole.astype(jnp.int32))
    steps = jnp.arange(need.shape[0], dtype=jnp.int32)
    latest = lax.cummax(jnp.where(need_b, steps, -1), axis=0)
    source = jnp.where(latest < 0, jnp.argmax(need_b).astype(jnp.int32), latest)
    kt = (jj + oo + REACH).astype(jnp.int32).reshape(-1)[source]
    qp = p_q[:, 0].astype(jnp.int32)
    kp = p_k.astype(jnp.int32).reshape(-1)[source]

    attended = flash(
        need, qp, kt, kp,
        own[0], kv_all[0], kv_all[1],
        seg_blocks.reshape(ctx_size, row_count, 1),
        seg_blocks.reshape(ctx_size, 1, row_count),
        score_scale,
    )

    slot_count = row_count // ctx_size
    dest_mine = dest_blocks[qp]
    place = (dest_mine // row_count) * slot_count + dest_mine % slot_count
    chooser = (
        place[:, None, :] == jnp.arange(row_count, dtype=jnp.int32)[None, :, None]
    ).astype(jnp.bfloat16)
    placed = jnp.einsum(
        "jsr,jrd->jsd", chooser, attended, preferred_element_type=jnp.float32
    ).astype(jnp.bfloat16)
    placed = placed.reshape(slots, ctx_size, slot_count, HD).transpose(1, 0, 2, 3)
    got = lax.all_to_all(placed, "ctx", split_axis=0, concat_axis=0, tiled=True)
    got = got.reshape(head_count, ctx_size, slot_count, HD).transpose(1, 2, 0, 3)
    owned_attended = got.reshape(row_count, row_width)

    wanted = (
        me * row_count
        + jnp.arange(ctx_size, dtype=jnp.int32)[:, None, None] * slot_count
        + jnp.arange(slot_count, dtype=jnp.int32)[None, :, None]
    )
    owned_video = jnp.sum(
        jnp.where(dest_blocks[:, None, :] == wanted, seg_blocks[:, None, :], 0), axis=2
    ).reshape(row_count)

    head_terms = jnp.dot(owned_attended, out_weight, preferred_element_type=jnp.float32)
    mixed_rows = lax.psum_scatter(
        head_terms.astype(jnp.bfloat16), "head", scatter_dimension=1, tiled=True
    ).astype(jnp.float32)
    video_gates = jnp.dot(
        jax.nn.one_hot(timestep, gate_table.shape[0], dtype=jnp.float32),
        gate_table,
        precision=lax.Precision.HIGHEST,
    )
    token_gates = jnp.dot(
        jax.nn.one_hot(owned_video, timestep.shape[0], dtype=jnp.float32),
        video_gates,
        precision=lax.Precision.HIGHEST,
    )
    return (mixed_rows * token_gates).astype(jnp.bfloat16)


def solution(mesh):
    placed = (
        P(("batch", "ctx"), "head"),
        P(("batch", "ctx"), "head"),
        P(("batch", "ctx"), "head"),
        P("head"),
        P("head"),
        P(("batch", "ctx")),
        P(("batch", "ctx")),
        P("batch"),
        P("head", None),
        P(None, "head"),
    )
    return jax.shard_map(
        local, mesh=mesh, in_specs=placed, out_specs=P(("batch", "ctx"), "head"), check_vma=False
    )
```

```python
import functools
import math

import jax
import jax.numpy as jnp
from jax import lax
from jax.experimental import pallas as pl
from jax.experimental.pallas import tpu as pltpu
from jax.sharding import PartitionSpec as P

HD = 128
REACH = 4


def flash_kernel(
    need_ref, qp_ref, kt_ref, kp_ref,
    q_ref, k_ref, v_ref, qs_ref, ks_ref,
    o_ref, m_scr, l_scr, acc_scr, *, offsets, score_scale
):
    j = pl.program_id(0)
    o = pl.program_id(1)

    @pl.when(o == 0)
    def _():
        m_scr[...] = jnp.full_like(m_scr, -1e30)
        l_scr[...] = jnp.zeros_like(l_scr)
        acc_scr[...] = jnp.zeros_like(acc_scr)

    def step(masked):
        q = q_ref[0]
        k = k_ref[0]
        s = lax.dot_general(
            q, k, (((1,), (1,)), ((), ())), preferred_element_type=jnp.float32
        ) * score_scale
        if masked:
            mask = qs_ref[0] == ks_ref[0]
            s = jnp.where(mask, s, -jnp.inf)
        m_prev = m_scr[...]
        m_new = jnp.maximum(m_prev, jnp.max(s, axis=1, keepdims=True))
        alpha = jnp.exp(m_prev - m_new)
        p = jnp.exp(s - m_new[:, :1])
        l_scr[...] = alpha * l_scr[...] + jnp.sum(p, axis=1, keepdims=True)
        acc_scr[...] = alpha * acc_scr[...] + jnp.dot(
            p.astype(jnp.bfloat16), v_ref[0], preferred_element_type=jnp.float32
        )
        m_scr[...] = m_new

    @pl.when(need_ref[j * offsets + o] == 1)
    def _():
        step(True)

    @pl.when(need_ref[j * offsets + o] == 2)
    def _():
        step(False)

    @pl.when(o == offsets - 1)
    def _():
        o_ref[0] = (acc_scr[...] / l_scr[...]).astype(o_ref.dtype)


def flash(need, qp, kt, kp, q_tiles, k_tiles, v_tiles, seg_rows, seg_cols, score_scale):
    slots, rows, width = q_tiles.shape
    offsets = 2 * REACH + 1
    kern = functools.partial(flash_kernel, offsets=offsets, score_scale=score_scale)
    grid_spec = pltpu.PrefetchScalarGridSpec(
        num_scalar_prefetch=4,
        grid=(slots, offsets),
        in_specs=[
            pl.BlockSpec((1, rows, width), lambda j, o, nd, qp, kt, kp: (j, 0, 0)),
            pl.BlockSpec((1, rows, width), lambda j, o, nd, qp, kt, kp: (kt[j * offsets + o], 0, 0)),
            pl.BlockSpec((1, rows, width), lambda j, o, nd, qp, kt, kp: (kt[j * offsets + o], 0, 0)),
            pl.BlockSpec((1, rows, 1), lambda j, o, nd, qp, kt, kp: (qp[j], 0, 0)),
            pl.BlockSpec((1, 1, rows), lambda j, o, nd, qp, kt, kp: (kp[j * offsets + o], 0, 0)),
        ],
        out_specs=pl.BlockSpec((1, rows, width), lambda j, o, nd, qp, kt, kp: (j, 0, 0)),
        scratch_shapes=[
            pltpu.VMEM((rows, width), jnp.float32),
            pltpu.VMEM((rows, width), jnp.float32),
            pltpu.VMEM((rows, width), jnp.float32),
        ],
    )
    return pl.pallas_call(
        kern,
        grid_spec=grid_spec,
        out_shape=jax.ShapeDtypeStruct((slots, rows, width), jnp.bfloat16),
        compiler_params=pltpu.CompilerParams(
            dimension_semantics=("arbitrary", "arbitrary")
        ),
    )(need, qp, kt, kp, q_tiles, k_tiles, v_tiles, seg_rows, seg_cols)


def relay_kernel(src_ref, mark_ref, dst_ref, marks_ref, send_sem, recv_sem, mark_send, mark_recv, self_sem,
                 *, slots, size, inverse):
    me = lax.axis_index("ctx")
    barrier = pltpu.get_barrier_semaphore()
    for step in range(1, size):
        pl.semaphore_signal(
            barrier, inc=1, device_id={"ctx": lax.rem(me + step, size)},
            device_id_type=pl.DeviceIdType.MESH,
        )
    pl.semaphore_wait(barrier, size - 1)
    copies = []
    for j in range(slots):
        target = lax.rem(inverse * (me - j + size), size)
        head = (slots * target + j) // size
        remote = pltpu.make_async_remote_copy(
            src_ref.at[head], dst_ref.at[j], send_sem.at[j], recv_sem.at[j],
            device_id={"ctx": target}, device_id_type=pl.DeviceIdType.MESH,
        )
        here = pltpu.make_async_copy(src_ref.at[head], dst_ref.at[j], recv_sem.at[j])
        is_self = target == me

        @pl.when(is_self)
        def _():
            here.start()

        @pl.when(jnp.logical_not(is_self))
        def _():
            remote.start()

        copies.append((remote, here, is_self))
    mark_copies = []
    for step in range(1, size):
        sent = pltpu.make_async_remote_copy(
            mark_ref, marks_ref.at[me], mark_send.at[step - 1], mark_recv.at[step - 1],
            device_id={"ctx": lax.rem(me + step, size)}, device_id_type=pl.DeviceIdType.MESH,
        )
        sent.start()
        mark_copies.append(sent)
    mine = pltpu.make_async_copy(mark_ref, marks_ref.at[me], self_sem.at[0])
    mine.start()
    for remote, here, is_self in copies:
        @pl.when(is_self)
        def _():
            here.wait()

        @pl.when(jnp.logical_not(is_self))
        def _():
            remote.wait_send()
            remote.wait_recv()

    for sent in mark_copies:
        sent.wait_send()
        sent.wait_recv()
    mine.wait()


def relay(tiles, marks, slots, size):
    inverse = pow(slots, -1, size)
    kern = functools.partial(relay_kernel, slots=slots, size=size, inverse=inverse)
    return pl.pallas_call(
        kern,
        out_shape=(
            jax.ShapeDtypeStruct((slots,) + tiles.shape[1:], tiles.dtype),
            jax.ShapeDtypeStruct((size,) + marks.shape, marks.dtype),
        ),
        in_specs=[pl.BlockSpec(memory_space=pl.ANY), pl.BlockSpec(memory_space=pl.ANY)],
        out_specs=(pl.BlockSpec(memory_space=pl.ANY), pl.BlockSpec(memory_space=pl.ANY)),
        scratch_shapes=[
            pltpu.SemaphoreType.DMA((slots,)),
            pltpu.SemaphoreType.DMA((slots,)),
            pltpu.SemaphoreType.DMA((size - 1,)),
            pltpu.SemaphoreType.DMA((size - 1,)),
            pltpu.SemaphoreType.DMA((1,)),
        ],
        compiler_params=pltpu.CompilerParams(collective_id=0, has_side_effects=True),
    )(tiles, marks)


def local(
    query_raw,
    key_raw,
    value_rows,
    query_gain,
    key_gain,
    segment,
    destination,
    timestep,
    out_weight,
    gate_table,
):
    row_count = query_raw.shape[0]
    row_width = query_raw.shape[1]
    head_count = row_width // HD
    ctx_size = lax.axis_size("ctx")
    total_width = row_width * lax.axis_size("head")
    score_scale = 1.0 / math.sqrt(HD)
    me = lax.axis_index("ctx")
    tiles = head_count * ctx_size
    slots = tiles // ctx_size

    query_float = query_raw.astype(jnp.float32)
    key_float = key_raw.astype(jnp.float32)
    query_sum, key_sum = lax.psum(
        (jnp.sum(query_float * query_float, axis=1), jnp.sum(key_float * key_float, axis=1)), "head"
    )
    queries = (
        query_float * lax.rsqrt(query_sum / total_width + 1e-06)[:, None] * query_gain
    ).astype(jnp.bfloat16)
    normed_keys = (key_float * lax.rsqrt(key_sum / total_width + 1e-06)[:, None] * key_gain).astype(
        jnp.bfloat16
    )

    qkv = jnp.stack([queries, normed_keys, value_rows]).reshape(3, row_count, head_count, HD)
    qkv = jnp.transpose(qkv, (0, 2, 1, 3))

    came, marks = relay(
        jnp.transpose(qkv, (1, 0, 2, 3)), jnp.stack([segment, destination]), slots, ctx_size
    )
    seg_blocks = marks[:, 0]
    dest_blocks = marks[:, 1]
    own = jnp.transpose(came, (1, 0, 2, 3))

    kv_own = own[1:]
    left = lax.ppermute(
        kv_own[:, slots - REACH:], "ctx", [(e, e + 1) for e in range(ctx_size - 1)]
    )
    right = lax.ppermute(
        kv_own[:, :REACH], "ctx", [(e, e - 1) for e in range(1, ctx_size)]
    )
    kv_all = jnp.concatenate([left, kv_own, right], axis=1)

    seg_lo = seg_blocks[:, 0]
    seg_hi = seg_blocks[:, -1]

    offsets = 2 * REACH + 1
    jj = jnp.arange(slots, dtype=jnp.int32)[:, None]
    oo = jnp.arange(offsets, dtype=jnp.int32)[None, :] - REACH
    t_q = slots * me + jj
    t_k = t_q + oo
    p_q = t_q % ctx_size
    valid = (t_k >= 0) & (t_k < tiles)
    t_kc = jnp.clip(t_k, 0, tiles - 1)
    p_k = t_kc % ctx_size
    same_head = (t_kc // ctx_size) == (t_q // ctx_size)
    meet = (seg_lo[p_q] <= seg_hi[p_k]) & (seg_lo[p_k] <= seg_hi[p_q])
    need_b = (valid & same_head & meet).reshape(-1)
    whole = (
        (seg_lo[p_q] == seg_hi[p_q]) & (seg_lo[p_k] == seg_hi[p_k]) & (seg_lo[p_q] == seg_lo[p_k])
    ).reshape(-1)
    need = need_b.astype(jnp.int32) * (1 + whole.astype(jnp.int32))
    steps = jnp.arange(need.shape[0], dtype=jnp.int32)
    latest = lax.cummax(jnp.where(need_b, steps, -1), axis=0)
    source = jnp.where(latest < 0, jnp.argmax(need_b).astype(jnp.int32), latest)
    kt = (jj + oo + REACH).astype(jnp.int32).reshape(-1)[source]
    qp = p_q[:, 0].astype(jnp.int32)
    kp = p_k.astype(jnp.int32).reshape(-1)[source]

    attended = flash(
        need, qp, kt, kp,
        own[0], kv_all[0], kv_all[1],
        seg_blocks.reshape(ctx_size, row_count, 1),
        seg_blocks.reshape(ctx_size, 1, row_count),
        score_scale,
    )

    slot_count = row_count // ctx_size
    dest_mine = dest_blocks[qp]
    place = (dest_mine // row_count) * slot_count + dest_mine % slot_count
    chooser = (
        place[:, None, :] == jnp.arange(row_count, dtype=jnp.int32)[None, :, None]
    ).astype(jnp.bfloat16)
    placed = jnp.einsum(
        "jsr,jrd->jsd", chooser, attended, preferred_element_type=jnp.float32
    ).astype(jnp.bfloat16)
    placed = placed.reshape(slots, ctx_size, slot_count, HD).transpose(1, 0, 2, 3)
    got = lax.all_to_all(placed, "ctx", split_axis=0, concat_axis=0, tiled=True)
    got = got.reshape(head_count, ctx_size, slot_count, HD).transpose(1, 2, 0, 3)
    owned_attended = got.reshape(row_count, row_width)

    wanted = (
        me * row_count
        + jnp.arange(ctx_size, dtype=jnp.int32)[:, None, None] * slot_count
        + jnp.arange(slot_count, dtype=jnp.int32)[None, :, None]
    )
    owned_video = jnp.sum(
        jnp.where(dest_blocks[:, None, :] == wanted, seg_blocks[:, None, :], 0), axis=2
    ).reshape(row_count)

    head_terms = jnp.dot(owned_attended, out_weight, preferred_element_type=jnp.float32)
    mixed_rows = lax.psum_scatter(
        head_terms.astype(jnp.bfloat16), "head", scatter_dimension=1, tiled=True
    ).astype(jnp.float32)
    video_gates = jnp.dot(
        jax.nn.one_hot(timestep, gate_table.shape[0], dtype=jnp.float32),
        gate_table,
        precision=lax.Precision.HIGHEST,
    )
    token_gates = jnp.dot(
        jax.nn.one_hot(owned_video, timestep.shape[0], dtype=jnp.float32),
        video_gates,
        precision=lax.Precision.HIGHEST,
    )
    return (mixed_rows * token_gates).astype(jnp.bfloat16)


def solution(mesh):
    placed = (
        P(("batch", "ctx"), "head"),
        P(("batch", "ctx"), "head"),
        P(("batch", "ctx"), "head"),
        P("head"),
        P("head"),
        P(("batch", "ctx")),
        P(("batch", "ctx")),
        P("batch"),
        P("head", None),
        P(None, "head"),
    )
    return jax.shard_map(
        local, mesh=mesh, in_specs=placed, out_specs=P(("batch", "ctx"), "head"), check_vma=False
    )
```
